128 devices in a mesh: seq: 32 (over z, y, core), mp: 4 (over x).
Axes of the slice: x: 4, y: 4, z: 4, core: 2. Of those that a mesh axis runs over, the one named last changes fastest.
Arguments:
- token_ids: int32 [2, 4096], P(None, 'seq'), may hold values from 0 to 511, as said below
- pair_mask: int32 [4096], P('seq'), may hold values from 0 to 1
- embed_table: bfloat16 [512, 3, 4096], P(None, None, 'mp'), may hold values from -6 to 6
- conv_filter: bfloat16 [256, 128], P('mp'), may hold values from -0.9 to 1
- w_out: bfloat16 [4096, 4096], P('mp'), may hold values from -0.09375 to 0.09375
- w_qkv: bfloat16 [3, 32, 128, 128], P(None, 'mp'), may hold values from -0.61871843 to 0.61871843
Outputs:
- gram: float32 [32, 128, 128], P('mp', 'seq')
The draws below stay inside these ranges and needn't reach their ends.
Inputs may be any that keep to these rules, and one draw needn't show every extreme that they name: `token_ids`: row 1 equals row 0 at about half of the positions.
All inputs are finite; a program needn't handle non-finite values.
Results may differ from the reference program's by a relative error of at most 0.0074.
Values may be sent and summed in bfloat16 or wider, within the bound.
A program may use at most 128 MiB of HBM per device.

```python
import math
import jax
import jax.numpy as jnp
from jax import lax

TOK_DEV = 128
HEADS = 32
HEAD = 128
TAPS = 128
GROUP = 16
VOCAB = 512
CHANNELS = 4096
FILTERS = 256
LEN = 4096


def draw_token_ids(key, part):
    key_one, key_two, key_three, key_four = jax.random.split(jax.random.fold_in(key, 11), 4)
    drawn_count = VOCAB - 4
    base_ids = jax.random.randint(key_one, (LEN,), 0, drawn_count, dtype=jnp.int32)
    other_ids = jax.random.randint(key_two, (LEN,), 0, drawn_count, dtype=jnp.int32)
    flipped = jax.random.randint(key_three, (LEN,), 0, 2, dtype=jnp.int32) == 0
    contrast_ids = jnp.where(flipped, other_ids, base_ids)
    spot = jax.random.randint(key_four, (), 0, LEN - 2 * TOK_DEV, dtype=jnp.int32)
    positions = jnp.arange(LEN, dtype=jnp.int32)
    planted = jnp.where(positions == spot, 0, -1)
    planted = jnp.where(positions == LEN - TOK_DEV - 5, VOCAB - 4, planted)
    planted = jnp.where(positions == LEN - TOK_DEV - 1, VOCAB - 3, planted)
    planted = jnp.where(positions == LEN - 2, VOCAB - 2, planted)
    planted = jnp.where(positions == LEN - 1, VOCAB - 1, planted)
    both_rows = jnp.stack([base_ids, contrast_ids])
    return jnp.where(planted[None, :] >= 0, planted[None, :], both_rows).astype(jnp.int32)


def draw_pair_mask(key, part):
    key_one = jax.random.fold_in(key, 17)
    positions = jnp.arange(LEN, dtype=jnp.int32)
    threshold = 200 + 600 * positions // LEN
    picks = jax.random.randint(key_one, (LEN,), 0, 1000, dtype=jnp.int32)
    return (picks < threshold).astype(jnp.int32)


def draw_embed_table(key, part):
    key_one = jax.random.fold_in(jax.random.fold_in(key, 23), 0)
    return jnp.clip(jax.random.normal(key_one, (VOCAB, 3, CHANNELS), jnp.float32), -6.0, 6.0).astype(jnp.bfloat16)


def draw_conv_filter(key, part):
    key_one, key_two, key_three = jax.random.split(jax.random.fold_in(key, 31), 3)
    log_rate = jax.random.uniform(key_one, (FILTERS, 1), jnp.float32, math.log(1.0 / 400.0), math.log(1.0 / 30.0))
    decay_rate = jnp.exp(log_rate)
    lead_tap = jax.random.uniform(key_two, (FILTERS, 1), jnp.float32, 0.3, 1.0)
    lag_index = jnp.arange(TAPS, dtype=jnp.float32)[None, :]
    tail_taps = 0.3 * jnp.clip(jax.random.normal(key_three, (FILTERS, TAPS), jnp.float32), -3.0, 3.0) * jnp.exp(-decay_rate * lag_index)
    return jnp.where(lag_index == 0.0, lead_tap, tail_taps).astype(jnp.bfloat16)


def draw_w_qkv(key, part):
    key_one, key_two, key_three = jax.random.split(jax.random.fold_in(key, 41), 3)
    mat_shape = (HEADS, HEAD, HEAD)
    unit_scale = 1.0 / math.sqrt(HEAD)
    w_query = 1.3 * unit_scale * jnp.clip(jax.random.normal(key_one, mat_shape, jnp.float32), -4.0, 4.0)
    noise_part = 1.3 * unit_scale * jnp.clip(jax.random.normal(key_two, mat_shape, jnp.float32), -4.0, 4.0)
    w_value = unit_scale * jnp.clip(jax.random.normal(key_three, mat_shape, jnp.float32), -4.0, 4.0)
    w_key = noise_part
    return jnp.stack([w_query, w_key, w_value]).astype(jnp.bfloat16)


def shard_levels(rng, extent, pieces, low, top_value):
    factor_of, own = 1.0, jax.random.fold_in(rng, 6)
    for dim, blocks in pieces:
        heights = jnp.exp(jax.random.uniform(jax.random.fold_in(own, dim), (blocks,), jnp.float32, low / len(pieces), top_value / len(pieces)))
        factor_of = factor_of * jnp.repeat(heights, extent[dim] // blocks).reshape([-1 if axis == dim else 1 for axis in range(len(extent))])
    return factor_of


def noise(own_key, shape, deviation, reach, cuts=(), held_as=jnp.bfloat16):
    drawn = jax.random.normal(own_key, shape, jnp.float32) * deviation
    if len(cuts) > 0:
        drawn = shard_levels(own_key, shape, cuts, -0.22, 0.18) * drawn
    return jnp.clip(drawn, min=-reach, max=reach).astype(held_as)


def setup_inputs(seed: int = 0) -> dict:
    streams_of = jax.random.split(jax.random.key(seed), 7)
    token_ids = draw_token_ids(jax.random.fold_in(streams_of[6], 71), 0)
    pair_mask = draw_pair_mask(jax.random.fold_in(streams_of[6], 71), 0)
    embed_table = draw_embed_table(jax.random.fold_in(streams_of[6], 71), 0)
    conv_filter = draw_conv_filter(jax.random.fold_in(streams_of[6], 71), 0)
    w_out = noise(streams_of[4], (CHANNELS, CHANNELS), CHANNELS ** -0.5, 0.09375, ((0, 4),))
    w_qkv = draw_w_qkv(jax.random.fold_in(streams_of[6], 71), 0)
    return {"token_ids": token_ids, "pair_mask": pair_mask, "embed_table": embed_table, "conv_filter": conv_filter, "w_out": w_out, "w_qkv": w_qkv}


MASKED_SCORE = -1e+30

def reference(token_ids, pair_mask, embed_table, conv_filter, w_out, w_qkv):
    features = jnp.take(embed_table, token_ids, axis=0)
    gated = (features[:, :, 1].astype(jnp.float32) * features[:, :, 2].astype(jnp.float32)).astype(jnp.bfloat16)
    tap_table = jnp.repeat(conv_filter.astype(jnp.float32), GROUP, axis=0)
    padded = jnp.pad(gated.astype(jnp.float32), ((0, 0), (TAPS, 0), (0, 0)))

    def add_tap(tap_index, running):
        shifted = lax.dynamic_slice_in_dim(padded, TAPS - tap_index, LEN, 1)
        tap_weight = lax.dynamic_index_in_dim(tap_table, tap_index, 1, keepdims=False)
        return running + shifted * tap_weight[None, None, :]
    convolved = lax.fori_loop(0, TAPS, add_tap, jnp.zeros((2, LEN, CHANNELS), jnp.float32))
    hyena_out = (features[:, :, 0].astype(jnp.float32) * convolved).astype(jnp.bfloat16)
    mixed_out = jnp.dot(hyena_out.reshape(2 * LEN, CHANNELS), w_out, preferred_element_type=jnp.float32)
    mixed_heads = mixed_out.astype(jnp.bfloat16).reshape(2, LEN, HEADS, HEAD).astype(jnp.float32)
    projected = tuple((jnp.einsum('sthd,hde->hste', mixed_heads, w_qkv[which].astype(jnp.float32)).astype(jnp.bfloat16) for which in range(3)))
    mask_float = pair_mask.astype(jnp.float32)
    positions = jnp.arange(LEN, dtype=jnp.int32)
    causal = positions[:, None] >= positions[None, :]
    score_scale = 1.0 / math.sqrt(HEAD)

    def per_head(head_items):
        queries, keys, values = head_items
        scores = jnp.einsum('sqe,ske->sqk', queries.astype(jnp.float32), keys.astype(jnp.float32)) * score_scale
        row_max = lax.optimization_barrier(jnp.max(jnp.where(causal, scores, MASKED_SCORE), axis=-1, keepdims=True))
        weights = jnp.where(causal, jnp.exp(scores - row_max), 0.0)
        row_sum = lax.optimization_barrier(jnp.sum(weights, axis=-1, keepdims=True))
        probs = lax.optimization_barrier(weights.astype(jnp.bfloat16))
        attended = jnp.einsum('sqk,ske->sqe', probs.astype(jnp.float32), values.astype(jnp.float32)) / row_sum
        rounded = lax.optimization_barrier((attended[0] - attended[1]).astype(jnp.bfloat16))
        difference = rounded.astype(jnp.float32)
        kept_rows = difference * mask_float[:, None]
        return jnp.einsum('te,tf->ef', kept_rows, difference)
    gram_sum = lax.map(per_head, projected)
    kept_count = jnp.sum(mask_float)
    return gram_sum / jnp.maximum(kept_count, 1.0)
```

```python
import functools
import math

import jax
import jax.numpy as jnp
from jax import lax
from jax.experimental import pallas as pl
from jax.experimental.pallas import tpu as pltpu
from jax.sharding import PartitionSpec as P

F32 = jnp.float32
BF16 = jnp.bfloat16
MESH = pl.DeviceIdType.MESH
MASKED_SCORE = -1e30
TOK = 128
HEAD = 128
GROUP = 16
TILE = 256
CHUNK = 512


def dot(a, b):
    return jnp.dot(a, b, preferred_element_type=F32)


def dot_rows(a, b):
    return lax.dot_general(a, b, (((0,), (0,)), ((), ())), preferred_element_type=F32)


def dot_lanes(a, b):
    return lax.dot_general(a, b, (((1,), (1,)), ((), ())), preferred_element_type=F32)


def kernel(
    seq_n,
    mp_n,
    tok_ref,
    mask_ref,
    emb_hbm,
    filt_ref,
    w_hbm,
    wqkv_hbm,
    out_ref,
    emb,
    wbuf,
    wh,
    halo_tok,
    mask_all,
    frev,
    toep,
    gate_tab,
    feat0,
    win,
    hy,
    send1,
    recv1,
    send_r,
    send_l,
    recv_r,
    recv_l,
    chain_r,
    chain_l,
    own,
    mixed,
    kv,
    keys,
    vals,
    scores,
    kept,
    ex_send,
    ex_recv,
    gram_send,
    gram_recv,
    emb_sem,
    w_sem,
    wh_sem,
    halo_s,
    halo_r,
    mask_s,
    mask_r,
    s1_s,
    s1_r,
    sr_s,
    sr_r,
    sl_s,
    sl_r,
    a2a_s,
    a2a_r,
    ex_s,
    ex_r,
    gr_s,
    gr_r,
):
    me = lax.axis_index("seq")
    x = lax.axis_index("mp")
    right = lax.rem(x + 1, mp_n)
    left = lax.rem(x + mp_n - 1, mp_n)
    far = lax.rem(x + 2, mp_n)
    channels = emb.shape[2]
    pairs = 4
    my_pair = me // 8
    my_head = me // 4
    half = lax.rem(me // 2, 2)
    side = lax.rem(me, 2)
    partner = me + 1 - 2 * side
    next_seq = lax.rem(me + 1, seq_n)

    def peer(n):
        return lax.rem(me + n, seq_n)

    barrier = pltpu.get_barrier_semaphore()
    for other in (left, right):
        pl.semaphore_signal(barrier, inc=1, device_id={"mp": other}, device_id_type=MESH)

    def greet(n, carry):
        pl.semaphore_signal(barrier, inc=1, device_id={"seq": peer(n)}, device_id_type=MESH)
        return carry

    lax.fori_loop(1, seq_n, greet, 0)

    emb_copies = [
        pltpu.make_async_copy(emb_hbm.at[i], emb.at[i], emb_sem.at[i]) for i in range(3)
    ]
    for i in (1, 2, 0):
        emb_copies[i].start()
    w_copies = []
    dests = [d for _ in range(pairs) for d in (far, right, left)] + [x] * pairs
    steps = [n for n in range(pairs) for _ in range(3)] + list(range(pairs))
    for i, (d, n) in enumerate(zip(dests, steps)):
        pair = lax.rem(my_pair + n, pairs)
        col = pl.multiple_of(d * 1024 + pair * 256, 256)
        w_copies.append(
            pltpu.make_async_copy(w_hbm.at[:, pl.ds(col, 256)], wbuf.at[i], w_sem.at[i])
        )
    for copy in w_copies:
        copy.start()
    wh_copy = pltpu.make_async_copy(wqkv_hbm.at[:, my_head], wh, wh_sem)
    wh_copy.start()

    row_io = lax.broadcasted_iota(jnp.int32, (TOK, TOK), 0)
    col_io = lax.broadcasted_iota(jnp.int32, (TOK, TOK), 1)
    total_io = row_io + col_io
    reverse = jnp.where((total_io == 0) | (total_io == TOK), 1.0, 0.0).astype(BF16)
    frev[...] = dot(filt_ref[...], reverse)

    def build(g, carry):
        base = jnp.broadcast_to(frev[pl.ds(g, 1), :], (TOK, TOK))
        turned = pltpu.roll(base, 0, 1, stride=1, stride_axis=0)
        toep[g, :, 0:TOK] = jnp.where(col_io > row_io, turned, 0.0).astype(BF16)
        toep[g, :, TOK : 2 * TOK] = jnp.where(col_io <= row_io, turned, 0.0).astype(BF16)
        return carry

    lax.fori_loop(0, filt_ref.shape[0], build, 0)

    pl.semaphore_wait(barrier, seq_n + 1)

    halo = pltpu.make_async_remote_copy(
        src_ref=tok_ref,
        dst_ref=halo_tok,
        send_sem=halo_s,
        recv_sem=halo_r,
        device_id={"seq": next_seq},
        device_id_type=MESH,
    )
    halo.start()

    mask_own = pltpu.make_async_copy(mask_ref, mask_all.at[me], mask_r)
    mask_own.start()

    def send_mask(n, carry):
        pltpu.make_async_remote_copy(
            src_ref=mask_ref,
            dst_ref=mask_all.at[me],
            send_sem=mask_s,
            recv_sem=mask_r,
            device_id={"seq": peer(n)},
            device_id_type=MESH,
        ).start()
        return carry

    lax.fori_loop(1, seq_n, send_mask, 0)

    vocab = emb.shape[1]
    vocab_io = lax.broadcasted_iota(jnp.int32, (vocab, TOK), 0)

    def onehot(ids_ref):
        hot = [
            jnp.where(vocab_io == jnp.broadcast_to(ids_ref[s : s + 1, :], (vocab, TOK)), 1.0, 0.0)
            for s in range(2)
        ]
        return jnp.concatenate(hot, axis=1).astype(BF16)

    emb_copies[1].wait()
    emb_copies[2].wait()
    gate_tab[...] = (emb[1].astype(F32) * emb[2].astype(F32)).astype(BF16)
    own_hot = onehot(tok_ref)
    emb_copies[0].wait()
    feat0[...] = dot_rows(own_hot, emb[0])
    current = dot_rows(own_hot, gate_tab[...]).astype(BF16)
    lane_tiles = channels // 128
    for c in range(lane_tiles):
        for s in range(2):
            win[c, TOK : 2 * TOK, s * 128 : (s + 1) * 128] = current[
                s * TOK : (s + 1) * TOK, c * 128 : (c + 1) * 128
            ]
    halo.wait()
    before = dot_rows(onehot(halo_tok), gate_tab[...])
    before = jnp.where(me > 0, before, 0.0).astype(BF16)
    for c in range(lane_tiles):
        for s in range(2):
            win[c, 0:TOK, s * 128 : (s + 1) * 128] = before[
                s * TOK : (s + 1) * TOK, c * 128 : (c + 1) * 128
            ]

    groups = 128 // GROUP
    lane_group = lax.rem(lax.broadcasted_iota(jnp.int32, (TOK, 256), 1), 128) // GROUP

    def convolve(c, carry):
        taps = toep[pl.ds(c * groups, groups)].reshape(groups * TOK, 2 * TOK)
        every = dot(taps, win[c])
        conv = every[0:TOK]
        for g in range(1, groups):
            conv = jnp.where(lane_group == g, every[g * TOK : (g + 1) * TOK], conv)
        lanes = pl.ds(pl.multiple_of(c * 128, 128), 128)
        for s in range(2):
            rows = pl.ds(s * TOK, TOK)
            hy[rows, lanes] = (feat0[rows, lanes] * conv[:, s * 128 : (s + 1) * 128]).astype(BF16)
        return carry

    lax.fori_loop(0, lane_tiles, convolve, 0)

    def part(i):
        w_copies[i].wait()
        return dot(hy[...], wbuf[i])

    def to_side(src, dst, ssem, rsem, other):
        copy = pltpu.make_async_remote_copy(
            src_ref=src,
            dst_ref=dst,
            send_sem=ssem,
            recv_sem=rsem,
            device_id={"mp": other},
            device_id_type=MESH,
        )
        copy.start()
        return copy

    first, second = {}, {}
    for n in range(pairs):
        p_far = part(3 * n)
        for h, other in ((0, right), (1, left)):
            send1[n, h] = p_far[:, h * HEAD : (h + 1) * HEAD].astype(BF16)
            first[n, h] = to_side(
                send1.at[n, h], recv1.at[n, h], s1_s.at[n, h], s1_r.at[n, h], other
            )
        p_right = part(3 * n + 1)
        chain_r[n] = p_right[:, :HEAD]
        send_r[n, 1] = p_right[:, HEAD:].astype(BF16)
        second[n, "r", 1] = to_side(
            send_r.at[n, 1], recv_l.at[n, 1], sr_s.at[n, 1], sr_r.at[n, 1], right
        )
        p_left = part(3 * n + 2)
        chain_l[n] = p_left[:, HEAD:]
        send_l[n, 0] = p_left[:, :HEAD].astype(BF16)
        second[n, "l", 0] = to_side(
            send_l.at[n, 0], recv_r.at[n, 0], sl_s.at[n, 0], sl_r.at[n, 0], left
        )
    for n in range(pairs):
        own[n] = part(12 + n)
        first[n, 0].wait()
        send_r[n, 0] = (chain_r[n] + recv1[n, 0].astype(F32)).astype(BF16)
        second[n, "r", 0] = to_side(
            send_r.at[n, 0], recv_l.at[n, 0], sr_s.at[n, 0], sr_r.at[n, 0], right
        )
        first[n, 1].wait()
        send_l[n, 1] = (chain_l[n] + recv1[n, 1].astype(F32)).astype(BF16)
        second[n, "l", 1] = to_side(
            send_l.at[n, 1], recv_r.at[n, 1], sl_s.at[n, 1], sl_r.at[n, 1], left
        )

    def deliver(n, r):
        member = lax.rem(lax.rem(me, 8) + r, 8)
        target = lax.rem(my_pair + n, pairs) * 8 + member
        return mixed.at[n, member // 4, lax.rem(member, 2)], target

    for n in range(pairs):
        for key in (("r", 1), ("l", 0), ("r", 0), ("l", 1)):
            second[(n,) + key].wait()
        for h in range(2):
            total = own[n, :, h * HEAD : (h + 1) * HEAD]
            total = total + recv_l[n, h].astype(F32) + recv_r[n, h].astype(F32)
            total = total.astype(BF16)
            mixed[n, h, 0] = total[:TOK]
            mixed[n, h, 1] = total[TOK:]

        def send_rows(r, carry, n=n):
            src, target = deliver(n, r)
            pltpu.make_async_remote_copy(
                src_ref=src,
                dst_ref=kv.at[me],
                send_sem=a2a_s,
                recv_sem=a2a_r,
                device_id={"seq": target},
                device_id_type=MESH,
            ).start()
            return carry

        if n == 0:
            src, _ = deliver(0, 0)
            pltpu.make_async_copy(src, kv.at[me], a2a_r).start()
        lax.fori_loop(1 if n == 0 else 0, 8, send_rows, 0)

    pltpu.make_async_copy(kv, kv, a2a_r).wait()
    wh_copy.wait()

    w_kv = jnp.concatenate([wh[1], wh[2]], axis=1)
    rows_per = CHUNK // TOK

    def project(c, carry):
        rows = kv[pl.ds(c * rows_per, rows_per)].reshape(CHUNK, HEAD)
        both = dot(rows, w_kv).astype(BF16)
        keys[c] = both[:, :HEAD]
        vals[c] = both[:, HEAD:]
        return carry

    lax.fori_loop(0, seq_n * TOK // CHUNK, project, 0)

    scale = math.log2(math.e) / math.sqrt(HEAD)
    tiles = seq_n * TOK // TILE // 2

    def lane_max(s, best):
        for j in range(CHUNK // 128):
            best = jnp.maximum(best, s[:, j * 128 : (j + 1) * 128])
        return best

    ex_copies = [
        pltpu.make_async_remote_copy(
            src_ref=ex_send.at[j],
            dst_ref=ex_recv.at[j],
            send_sem=ex_s.at[j],
            recv_sem=ex_r.at[j],
            device_id={"seq": partner},
            device_id_type=MESH,
        )
        for j in range(tiles // 2)
    ]

    for n in range(tiles):
        tile = 2 * n + lax.rem(n + half, 2)
        q = dot(kv[pl.ds(2 * tile, 2)].reshape(TILE, HEAD), wh[0]).astype(BF16)

        def score(c, best):
            s = dot_lanes(q, keys[c])
            scores[c] = s
            return lane_max(s, best)

        best = jnp.full((TILE, 128), MASKED_SCORE, F32)
        if n > 0:
            best = lax.fori_loop(0, n, score, best)
        s = dot_lanes(q, keys[n])
        q_pos = tile * TILE + lax.broadcasted_iota(jnp.int32, (TILE, CHUNK), 0)
        k_pos = n * CHUNK + lax.broadcasted_iota(jnp.int32, (TILE, CHUNK), 1)
        s = jnp.where(k_pos <= q_pos, s, MASKED_SCORE)
        scores[n] = s
        top = jnp.max(lane_max(s, best), axis=1, keepdims=True)

        def weigh(c, state):
            row_sum, acc = state
            w = jnp.exp2((scores[c] - top) * scale)
            for j in range(CHUNK // 128):
                row_sum = row_sum + w[:, j * 128 : (j + 1) * 128]
            return row_sum, acc + dot(w.astype(BF16), vals[c])

        zero = jnp.zeros((TILE, HEAD), F32)
        row_sum, acc = lax.fori_loop(0, n + 1, weigh, (zero, zero))
        attended = acc / jnp.sum(row_sum, axis=1, keepdims=True)

        @pl.when(side == n % 2)
        def _(attended=attended, n=n):
            kept[n // 2] = attended

        @pl.when(side != n % 2)
        def _(attended=attended, n=n):
            ex_send[n // 2] = attended
            ex_copies[n // 2].start()

    pltpu.make_async_copy(mask_all, mask_all, mask_r).wait()
    gram = jnp.zeros((HEAD, HEAD), F32)
    for j in range(tiles // 2):
        ex_copies[j].wait()
        tile = 2 * (2 * j + side) + lax.rem(side + half, 2)
        diff = (kept[j] - ex_recv[j]).astype(BF16)
        chosen = jnp.concatenate(
            [mask_all[2 * tile].astype(F32), mask_all[2 * tile + 1].astype(F32)], axis=1
        )
        turned = (jnp.transpose(diff.astype(F32)) * chosen).astype(BF16)
        gram = gram + dot(turned, diff)

    rows_out = HEAD // seq_n
    for i in range(seq_n):
        gram_send[i] = gram[i * rows_out : (i + 1) * rows_out]
    pltpu.make_async_copy(gram_send.at[me], gram_recv.at[me], gr_r).start()

    def send_gram(n, carry):
        target = peer(n)
        pltpu.make_async_remote_copy(
            src_ref=gram_send.at[target],
            dst_ref=gram_recv.at[me],
            send_sem=gr_s,
            recv_sem=gr_r,
            device_id={"seq": target},
            device_id_type=MESH,
        ).start()
        return carry

    lax.fori_loop(1, seq_n, send_gram, 0)

    count = jnp.sum(jnp.sum(mask_all[...].astype(F32), axis=0), axis=1, keepdims=True)
    count = jnp.maximum(count, 1.0)
    pltpu.make_async_copy(gram_recv, gram_recv, gr_r).wait()
    for h in range(out_ref.shape[0]):
        total = gram_recv[4 * h] + gram_recv[4 * h + 1]
        total = total + (gram_recv[4 * h + 2] + gram_recv[4 * h + 3])
        out_ref[h] = total / count

    rest = seq_n - 1
    pltpu.make_async_copy(kv.at[pl.ds(0, rest)], kv.at[pl.ds(0, rest)], a2a_s).wait()
    pltpu.make_async_copy(mask_all.at[pl.ds(0, rest)], mask_all.at[pl.ds(0, rest)], mask_s).wait()
    pltpu.make_async_copy(gram_recv.at[pl.ds(0, rest)], gram_recv.at[pl.ds(0, rest)], gr_s).wait()


def body(seq_n, mp_n, token_ids, pair_mask, embed_table, conv_filter, w_out, w_qkv):
    vocab, _, channels = embed_table.shape
    filters = conv_filter.shape[0]
    heads = w_qkv.shape[1]
    length = seq_n * TOK
    chunks = length // CHUNK
    tiles = length // TILE // 2
    vmem = pl.BlockSpec(memory_space=pltpu.VMEM)
    hbm = pl.BlockSpec(memory_space=pl.ANY)
    dma = pltpu.SemaphoreType.DMA
    scratch = [
        pltpu.VMEM((3, vocab, channels), BF16),
        pltpu.VMEM((16, channels, 256), BF16),
        pltpu.VMEM((3, HEAD, HEAD), BF16),
        pltpu.VMEM((2, TOK), jnp.int32),
        pltpu.VMEM((seq_n, 1, TOK), jnp.int32),
        pltpu.VMEM((filters, TOK), F32),
        pltpu.VMEM((filters, TOK, 2 * TOK), BF16),
        pltpu.VMEM((vocab, channels), BF16),
        pltpu.VMEM((2 * TOK, channels), F32),
        pltpu.VMEM((channels // 128, 2 * TOK, 256), BF16),
        pltpu.VMEM((2 * TOK, channels), BF16),
        pltpu.VMEM((4, 2, 2 * TOK, HEAD), BF16),
        pltpu.VMEM((4, 2, 2 * TOK, HEAD), BF16),
        pltpu.VMEM((4, 2, 2 * TOK, HEAD), BF16),
        pltpu.VMEM((4, 2, 2 * TOK, HEAD), BF16),
        pltpu.VMEM((4, 2, 2 * TOK, HEAD), BF16),
        pltpu.VMEM((4, 2, 2 * TOK, HEAD), BF16),
        pltpu.VMEM((4, 2 * TOK, HEAD), F32),
        pltpu.VMEM((4, 2 * TOK, HEAD), F32),
        pltpu.VMEM((4, 2 * TOK, 2 * HEAD), F32),
        pltpu.VMEM((4, 2, 2, TOK, HEAD), BF16),
        pltpu.VMEM((seq_n, TOK, HEAD), BF16),
        pltpu.VMEM((chunks, CHUNK, HEAD), BF16),
        pltpu.VMEM((chunks, CHUNK, HEAD), BF16),
        pltpu.VMEM((chunks, TILE, CHUNK), F32),
        pltpu.VMEM((tiles // 2, TILE, HEAD), F32),
        pltpu.VMEM((tiles // 2, TILE, HEAD), F32),
        pltpu.VMEM((tiles // 2, TILE, HEAD), F32),
        pltpu.VMEM((seq_n, HEAD // seq_n, HEAD), F32),
        pltpu.VMEM((seq_n, HEAD // seq_n, HEAD), F32),
        dma((3,)),
        dma((16,)),
        dma,
        dma,
        dma,
        dma,
        dma,
        dma((4, 2)),
        dma((4, 2)),
        dma((4, 2)),
        dma((4, 2)),
        dma((4, 2)),
        dma((4, 2)),
        dma,
        dma,
        dma((tiles // 2,)),
        dma((tiles // 2,)),
        dma,
        dma,
    ]
    return pl.pallas_call(
        functools.partial(kernel, seq_n, mp_n),
        out_shape=jax.ShapeDtypeStruct((heads, HEAD // seq_n, HEAD), F32),
        in_specs=[vmem, vmem, hbm, vmem, hbm, hbm],
        out_specs=vmem,
        scratch_shapes=scratch,
        compiler_params=pltpu.CompilerParams(
            collective_id=0, has_side_effects=True, vmem_limit_bytes=56 * 1024 * 1024
        ),
        name="steer",
    )(
        token_ids,
        pair_mask.reshape(1, TOK),
        embed_table.transpose(1, 0, 2),
        conv_filter,
        w_out,
        w_qkv,
    )


def solution(mesh):
    in_specs = (
        P(None, "seq"),
        P("seq"),
        P(None, None, "mp"),
        P("mp", None),
        P("mp", None),
        P(None, "mp", None, None),
    )
    out_specs = P("mp", "seq", None)
    run = functools.partial(body, mesh.shape["seq"], mesh.shape["mp"])
    return jax.shard_map(run, mesh=mesh, in_specs=in_specs, out_specs=out_specs, check_vma=False)
```

```python
import functools
import math

import jax
import jax.numpy as jnp
from jax import lax
from jax.experimental import pallas as pl
from jax.experimental.pallas import tpu as pltpu
from jax.sharding import PartitionSpec as P

F32 = jnp.float32
BF16 = jnp.bfloat16
MESH = pl.DeviceIdType.MESH
MASKED_SCORE = -1e30
TOK = 128
HEAD = 128
GROUP = 16
TILE = 256
CHUNK = 512


def dot(a, b):
    return jnp.dot(a, b, preferred_element_type=F32)


def dot_rows(a, b):
    return lax.dot_general(a, b, (((0,), (0,)), ((), ())), preferred_element_type=F32)


def dot_lanes(a, b):
    return lax.dot_general(a, b, (((1,), (1,)), ((), ())), preferred_element_type=F32)


def kernel(
    seq_n,
    mp_n,
    tok_ref,
    mask_ref,
    emb_hbm,
    filt_ref,
    w_hbm,
    wqkv_hbm,
    out_ref,
    emb,
    wbuf,
    wh,
    halo_tok,
    mask_all,
    frev,
    toep,
    gate_tab,
    feat0,
    win,
    hy,
    send1,
    recv1,
    send_r,
    send_l,
    recv_r,
    recv_l,
    chain_r,
    chain_l,
    own,
    mixed,
    kv,
    keys,
    vals,
    queries,
    scores,
    kept,
    ex_send,
    ex_recv,
    gram_send,
    gram_recv,
    emb_sem,
    w_sem,
    wh_sem,
    halo_s,
    halo_r,
    mask_s,
    mask_r,
    s1_s,
    s1_r,
    sr_s,
    sr_r,
    sl_s,
    sl_r,
    a2a_s,
    a2a_r,
    ex_s,
    ex_r,
    gr_s,
    gr_r,
):
    me = lax.axis_index("seq")
    x = lax.axis_index("mp")
    right = lax.rem(x + 1, mp_n)
    left = lax.rem(x + mp_n - 1, mp_n)
    far = lax.rem(x + 2, mp_n)
    channels = emb.shape[2]
    pairs = 4
    my_pair = me // 8
    my_head = me // 4
    half = lax.rem(me // 2, 2)
    side = lax.rem(me, 2)
    partner = me + 1 - 2 * side
    next_seq = lax.rem(me + 1, seq_n)

    def peer(n):
        return lax.rem(me + n, seq_n)

    barrier = pltpu.get_barrier_semaphore()
    for other in (left, right):
        pl.semaphore_signal(barrier, inc=1, device_id={"mp": other}, device_id_type=MESH)

    def greet(n, carry):
        pl.semaphore_signal(barrier, inc=1, device_id={"seq": peer(n)}, device_id_type=MESH)
        return carry

    lax.fori_loop(1, seq_n, greet, 0)

    emb_copies = [
        pltpu.make_async_copy(emb_hbm.at[i], emb.at[i], emb_sem.at[i]) for i in range(3)
    ]
    for i in (1, 2, 0):
        emb_copies[i].start()
    w_copies = []
    dests = [d for _ in range(pairs) for d in (far, right, left)] + [x] * pairs
    steps = [n for n in range(pairs) for _ in range(3)] + list(range(pairs))
    order = (0, 1, 2, 3, 12, 4, 5, 6, 13, 7, 8, 9, 14, 10, 11, 15)
    for i, (d, n) in enumerate(zip(dests, steps)):
        pair = lax.rem(my_pair + n, pairs)
        col = pl.multiple_of(d * 1024 + pair * 256, 256)
        w_copies.append(
            pltpu.make_async_copy(w_hbm.at[:, pl.ds(col, 256)], wbuf.at[i], w_sem.at[i])
        )
    for i in order:
        w_copies[i].start()
    wh_copy = pltpu.make_async_copy(wqkv_hbm.at[:, my_head], wh, wh_sem)
    wh_copy.start()

    row_io = lax.broadcasted_iota(jnp.int32, (TOK, TOK), 0)
    col_io = lax.broadcasted_iota(jnp.int32, (TOK, TOK), 1)
    total_io = row_io + col_io
    reverse = jnp.where((total_io == 0) | (total_io == TOK), 1.0, 0.0).astype(BF16)
    frev[...] = dot(filt_ref[...], reverse)

    def build(g, carry):
        base = jnp.broadcast_to(frev[pl.ds(g, 1), :], (TOK, TOK))
        turned = pltpu.roll(base, 0, 1, stride=1, stride_axis=0)
        toep[g, :, 0:TOK] = jnp.where(col_io > row_io, turned, 0.0).astype(BF16)
        toep[g, :, TOK : 2 * TOK] = jnp.where(col_io <= row_io, turned, 0.0).astype(BF16)
        return carry

    lax.fori_loop(0, filt_ref.shape[0], build, 0)

    pl.semaphore_wait(barrier, seq_n + 1)

    halo = pltpu.make_async_remote_copy(
        src_ref=tok_ref,
        dst_ref=halo_tok,
        send_sem=halo_s,
        recv_sem=halo_r,
        device_id={"seq": next_seq},
        device_id_type=MESH,
    )
    halo.start()

    mask_own = pltpu.make_async_copy(mask_ref, mask_all.at[me], mask_r)
    mask_own.start()

    def send_mask(n, carry):
        pltpu.make_async_remote_copy(
            src_ref=mask_ref,
            dst_ref=mask_all.at[me],
            send_sem=mask_s,
            recv_sem=mask_r,
            device_id={"seq": peer(n)},
            device_id_type=MESH,
        ).start()
        return carry

    lax.fori_loop(1, seq_n, send_mask, 0)

    vocab = emb.shape[1]
    vocab_io = lax.broadcasted_iota(jnp.int32, (vocab, TOK), 0)

    def onehot(ids_ref):
        hot = [
            jnp.where(vocab_io == jnp.broadcast_to(ids_ref[s : s + 1, :], (vocab, TOK)), 1.0, 0.0)
            for s in range(2)
        ]
        return jnp.concatenate(hot, axis=1).astype(BF16)

    emb_copies[1].wait()
    emb_copies[2].wait()
    gate_tab[...] = (emb[1].astype(F32) * emb[2].astype(F32)).astype(BF16)
    own_hot = onehot(tok_ref)
    emb_copies[0].wait()
    feat0[...] = dot_rows(own_hot, emb[0])
    current = dot_rows(own_hot, gate_tab[...]).astype(BF16)
    lane_tiles = channels // 128
    for c in range(lane_tiles):
        for s in range(2):
            win[c, TOK : 2 * TOK, s * 128 : (s + 1) * 128] = current[
                s * TOK : (s + 1) * TOK, c * 128 : (c + 1) * 128
            ]
    halo.wait()
    before = dot_rows(onehot(halo_tok), gate_tab[...])
    before = jnp.where(me > 0, before, 0.0).astype(BF16)
    for c in range(lane_tiles):
        for s in range(2):
            win[c, 0:TOK, s * 128 : (s + 1) * 128] = before[
                s * TOK : (s + 1) * TOK, c * 128 : (c + 1) * 128
            ]

    groups = 128 // GROUP
    lane_group = lax.rem(lax.broadcasted_iota(jnp.int32, (TOK, 256), 1), 128) // GROUP

    def convolve(c, carry):
        taps = toep[pl.ds(c * groups, groups)].reshape(groups * TOK, 2 * TOK)
        every = dot(taps, win[c])
        conv = every[0:TOK]
        for g in range(1, groups):
            conv = jnp.where(lane_group == g, every[g * TOK : (g + 1) * TOK], conv)
        lanes = pl.ds(pl.multiple_of(c * 128, 128), 128)
        for s in range(2):
            rows = pl.ds(s * TOK, TOK)
            hy[rows, lanes] = (feat0[rows, lanes] * conv[:, s * 128 : (s + 1) * 128]).astype(BF16)
        return carry

    lax.fori_loop(0, lane_tiles, convolve, 0)

    def part(i):
        w_copies[i].wait()
        return dot(hy[...], wbuf[i])

    def to_side(src, dst, ssem, rsem, other):
        copy = pltpu.make_async_remote_copy(
            src_ref=src,
            dst_ref=dst,
            send_sem=ssem,
            recv_sem=rsem,
            device_id={"mp": other},
            device_id_type=MESH,
        )
        copy.start()
        return copy

    first, second = {}, {}

    def send_far(n):
        p_far = part(3 * n)
        for h, other in ((0, right), (1, left)):
            send1[n, h] = p_far[:, h * HEAD : (h + 1) * HEAD].astype(BF16)
            first[n, h] = to_side(
                send1.at[n, h], recv1.at[n, h], s1_s.at[n, h], s1_r.at[n, h], other
            )

    def send_near(n):
        p_right = part(3 * n + 1)
        p_left = part(3 * n + 2)
        send_r[n, 1] = p_right[:, HEAD:].astype(BF16)
        second[n, "r", 1] = to_side(
            send_r.at[n, 1], recv_l.at[n, 1], sr_s.at[n, 1], sr_r.at[n, 1], right
        )
        send_l[n, 0] = p_left[:, :HEAD].astype(BF16)
        second[n, "l", 0] = to_side(
            send_l.at[n, 0], recv_r.at[n, 0], sl_s.at[n, 0], sl_r.at[n, 0], left
        )
        chain_r[n] = p_right[:, :HEAD]
        chain_l[n] = p_left[:, HEAD:]

    def send_chain(n):
        first[n, 0].wait()
        send_r[n, 0] = (chain_r[n] + recv1[n, 0].astype(F32)).astype(BF16)
        second[n, "r", 0] = to_side(
            send_r.at[n, 0], recv_l.at[n, 0], sr_s.at[n, 0], sr_r.at[n, 0], right
        )
        first[n, 1].wait()
        send_l[n, 1] = (chain_l[n] + recv1[n, 1].astype(F32)).astype(BF16)
        second[n, "l", 1] = to_side(
            send_l.at[n, 1], recv_r.at[n, 1], sl_s.at[n, 1], sl_r.at[n, 1], left
        )
        own[n] = part(12 + n)

    def deliver(n, r):
        member = lax.rem(lax.rem(me, 8) + r, 8)
        target = lax.rem(my_pair + n, pairs) * 8 + member
        return mixed.at[n, member // 4, lax.rem(member, 2)], target

    def spread(n):
        for key in (("r", 1), ("l", 0), ("r", 0), ("l", 1)):
            second[(n,) + key].wait()
        for h in range(2):
            total = own[n, :, h * HEAD : (h + 1) * HEAD]
            total = total + recv_l[n, h].astype(F32) + recv_r[n, h].astype(F32)
            total = total.astype(BF16)
            mixed[n, h, 0] = total[:TOK]
            mixed[n, h, 1] = total[TOK:]

        def send_rows(r, carry, n=n):
            src, target = deliver(n, r)
            pltpu.make_async_remote_copy(
                src_ref=src,
                dst_ref=kv.at[me],
                send_sem=a2a_s,
                recv_sem=a2a_r,
                device_id={"seq": target},
                device_id_type=MESH,
            ).start()
            return carry

        if n == 0:
            src, _ = deliver(0, 0)
            pltpu.make_async_copy(src, kv.at[me], a2a_r).start()
        lax.fori_loop(1 if n == 0 else 0, 8, send_rows, 0)

    send_far(0)
    send_near(0)
    send_far(1)
    for n in range(pairs):
        send_chain(n)
        if n + 1 < pairs:
            send_near(n + 1)
        if n + 2 < pairs:
            send_far(n + 2)
        if n > 0:
            spread(n - 1)
    spread(pairs - 1)

    pltpu.make_async_copy(kv, kv, a2a_r).wait()
    wh_copy.wait()

    rows_per = CHUNK // TOK

    def project(c, carry):
        rows = kv[pl.ds(c * rows_per, rows_per)].reshape(CHUNK, HEAD)
        keys[c] = dot(rows, wh[1]).astype(BF16)
        vals[c] = lax.dot_general(
            wh[2], rows, (((0,), (1,)), ((), ())), preferred_element_type=F32
        ).astype(BF16)
        return carry

    lax.fori_loop(0, seq_n * TOK // CHUNK, project, 0)

    scale = math.log2(math.e) / math.sqrt(HEAD)
    tiles = seq_n * TOK // TILE // 2

    def tile_of(n):
        return 2 * n + lax.rem(n + half, 2)

    for n in range(tiles):
        rows = kv[pl.ds(2 * tile_of(n), 2)].reshape(TILE, HEAD)
        queries[n] = dot(rows, wh[0]).astype(BF16)

    def fold(s):
        return s.reshape(CHUNK // 8, 8, TILE)

    ex_copies = [
        pltpu.make_async_remote_copy(
            src_ref=ex_send.at[j],
            dst_ref=ex_recv.at[j],
            send_sem=ex_s.at[j],
            recv_sem=ex_r.at[j],
            device_id={"seq": partner},
            device_id_type=MESH,
        )
        for j in range(tiles // 2)
    ]

    low = jnp.full((8, TILE), MASKED_SCORE, F32)
    best = low
    for n in range(tiles):
        s = dot_lanes(keys[n], queries[n])
        q_pos = tile_of(n) * TILE + lax.broadcasted_iota(jnp.int32, (CHUNK, TILE), 1)
        k_pos = n * CHUNK + lax.broadcasted_iota(jnp.int32, (CHUNK, TILE), 0)
        s = jnp.where(k_pos <= q_pos, s, MASKED_SCORE)
        scores[n % 2, n] = s
        best = jnp.maximum(best, jnp.max(fold(s), axis=0))
        top = jnp.max(best, axis=0, keepdims=True)
        best = low
        row_sum = jnp.zeros((8, TILE), F32)
        acc = jnp.zeros((HEAD, TILE), F32)
        for c in range(n + 1):
            w = jnp.exp2((scores[n % 2, c] - top) * scale)
            row_sum = row_sum + jnp.sum(fold(w), axis=0)
            acc = acc + dot(vals[c], w.astype(BF16))
            if n + 1 < tiles:
                s = dot_lanes(keys[c], queries[n + 1])
                scores[(n + 1) % 2, c] = s
                best = jnp.maximum(best, jnp.max(fold(s), axis=0))
        attended = acc / jnp.sum(row_sum, axis=0, keepdims=True)

        @pl.when(side == n % 2)
        def _(attended=attended, n=n):
            kept[n // 2] = attended

        @pl.when(side != n % 2)
        def _(attended=attended, n=n):
            ex_send[n // 2] = attended
            ex_copies[n // 2].start()

    pltpu.make_async_copy(mask_all, mask_all, mask_r).wait()
    gram = jnp.zeros((HEAD, HEAD), F32)
    for j in range(tiles // 2):
        ex_copies[j].wait()
        tile = 2 * (2 * j + side) + lax.rem(side + half, 2)
        diff = (kept[j] - ex_recv[j]).astype(BF16)
        chosen = jnp.concatenate(
            [mask_all[2 * tile].astype(F32), mask_all[2 * tile + 1].astype(F32)], axis=1
        )
        gram = gram + dot_lanes((diff.astype(F32) * chosen).astype(BF16), diff)

    rows_out = HEAD // seq_n
    for i in range(seq_n):
        gram_send[i] = gram[i * rows_out : (i + 1) * rows_out]
    pltpu.make_async_copy(gram_send.at[me], gram_recv.at[me], gr_r).start()

    def send_gram(n, carry):
        target = peer(n)
        pltpu.make_async_remote_copy(
            src_ref=gram_send.at[target],
            dst_ref=gram_recv.at[me],
            send_sem=gr_s,
            recv_sem=gr_r,
            device_id={"seq": target},
            device_id_type=MESH,
        ).start()
        return carry

    lax.fori_loop(1, seq_n, send_gram, 0)

    count = jnp.sum(jnp.sum(mask_all[...].astype(F32), axis=0), axis=1, keepdims=True)
    count = jnp.maximum(count, 1.0)
    pltpu.make_async_copy(gram_recv, gram_recv, gr_r).wait()
    for h in range(out_ref.shape[0]):
        total = gram_recv[4 * h] + gram_recv[4 * h + 1]
        total = total + (gram_recv[4 * h + 2] + gram_recv[4 * h + 3])
        out_ref[h] = total / count

    rest = seq_n - 1
    pltpu.make_async_copy(kv.at[pl.ds(0, rest)], kv.at[pl.ds(0, rest)], a2a_s).wait()
    pltpu.make_async_copy(mask_all.at[pl.ds(0, rest)], mask_all.at[pl.ds(0, rest)], mask_s).wait()
    pltpu.make_async_copy(gram_recv.at[pl.ds(0, rest)], gram_recv.at[pl.ds(0, rest)], gr_s).wait()


def body(seq_n, mp_n, token_ids, pair_mask, embed_table, conv_filter, w_out, w_qkv):
    vocab, _, channels = embed_table.shape
    filters = conv_filter.shape[0]
    heads = w_qkv.shape[1]
    length = seq_n * TOK
    chunks = length // CHUNK
    tiles = length // TILE // 2
    vmem = pl.BlockSpec(memory_space=pltpu.VMEM)
    hbm = pl.BlockSpec(memory_space=pl.ANY)
    dma = pltpu.SemaphoreType.DMA
    scratch = [
        pltpu.VMEM((3, vocab, channels), BF16),
        pltpu.VMEM((16, channels, 256), BF16),
        pltpu.VMEM((3, HEAD, HEAD), BF16),
        pltpu.VMEM((2, TOK), jnp.int32),
        pltpu.VMEM((seq_n, 1, TOK), jnp.int32),
        pltpu.VMEM((filters, TOK), F32),
        pltpu.VMEM((filters, TOK, 2 * TOK), BF16),
        pltpu.VMEM((vocab, channels), BF16),
        pltpu.VMEM((2 * TOK, channels), F32),
        pltpu.VMEM((channels // 128, 2 * TOK, 256), BF16),
        pltpu.VMEM((2 * TOK, channels), BF16),
        pltpu.VMEM((4, 2, 2 * TOK, HEAD), BF16),
        pltpu.VMEM((4, 2, 2 * TOK, HEAD), BF16),
        pltpu.VMEM((4, 2, 2 * TOK, HEAD), BF16),
        pltpu.VMEM((4, 2, 2 * TOK, HEAD), BF16),
        pltpu.VMEM((4, 2, 2 * TOK, HEAD), BF16),
        pltpu.VMEM((4, 2, 2 * TOK, HEAD), BF16),
        pltpu.VMEM((4, 2 * TOK, HEAD), F32),
        pltpu.VMEM((4, 2 * TOK, HEAD), F32),
        pltpu.VMEM((4, 2 * TOK, 2 * HEAD), F32),
        pltpu.VMEM((4, 2, 2, TOK, HEAD), BF16),
        pltpu.VMEM((seq_n, TOK, HEAD), BF16),
        pltpu.VMEM((chunks, CHUNK, HEAD), BF16),
        pltpu.VMEM((chunks, HEAD, CHUNK), BF16),
        pltpu.VMEM((tiles, TILE, HEAD), BF16),
        pltpu.VMEM((2, chunks, CHUNK, TILE), F32),
        pltpu.VMEM((tiles // 2, HEAD, TILE), F32),
        pltpu.VMEM((tiles // 2, HEAD, TILE), F32),
        pltpu.VMEM((tiles // 2, HEAD, TILE), F32),
        pltpu.VMEM((seq_n, HEAD // seq_n, HEAD), F32),
        pltpu.VMEM((seq_n, HEAD // seq_n, HEAD), F32),
        dma((3,)),
        dma((16,)),
        dma,
        dma,
        dma,
        dma,
        dma,
        dma((4, 2)),
        dma((4, 2)),
        dma((4, 2)),
        dma((4, 2)),
        dma((4, 2)),
        dma((4, 2)),
        dma,
        dma,
        dma((tiles // 2,)),
        dma((tiles // 2,)),
        dma,
        dma,
    ]
    return pl.pallas_call(
        functools.partial(kernel, seq_n, mp_n),
        out_shape=jax.ShapeDtypeStruct((heads, HEAD // seq_n, HEAD), F32),
        in_specs=[vmem, vmem, hbm, vmem, hbm, hbm],
        out_specs=vmem,
        scratch_shapes=scratch,
        compiler_params=pltpu.CompilerParams(
            collective_id=0, has_side_effects=True, vmem_limit_bytes=56 * 1024 * 1024
        ),
        name="steer",
    )(
        token_ids,
        pair_mask.reshape(1, TOK),
        embed_table.transpose(1, 0, 2),
        conv_filter,
        w_out,
        w_qkv,
    )


def solution(mesh):
    in_specs = (
        P(None, "seq"),
        P("seq"),
        P(None, None, "mp"),
        P("mp", None),
        P("mp", None),
        P(None, "mp", None, None),
    )
    out_specs = P("mp", "seq", None)
    run = functools.partial(body, mesh.shape["seq"], mesh.shape["mp"])
    return jax.shard_map(run, mesh=mesh, in_specs=in_specs, out_specs=out_specs, check_vma=False)
```

```python
import functools
import math

import jax
import jax.numpy as jnp
from jax import lax
from jax.experimental import pallas as pl
from jax.experimental.pallas import tpu as pltpu
from jax.sharding import PartitionSpec as P

F32 = jnp.float32
BF16 = jnp.bfloat16
MESH = pl.DeviceIdType.MESH
MASKED_SCORE = -1e30
TOK = 128
HEAD = 128
GROUP = 16
TILE = 256
CHUNK = 512
OFFSETS = (2, 1, 3, 0)


def dot(a, b):
    return jnp.dot(a, b, preferred_element_type=F32)


def dot_rows(a, b):
    return lax.dot_general(a, b, (((0,), (0,)), ((), ())), preferred_element_type=F32)


def dot_lanes(a, b):
    return lax.dot_general(a, b, (((1,), (1,)), ((), ())), preferred_element_type=F32)


def kernel(
    seq_n,
    mp_n,
    tok_ref,
    mask_ref,
    emb_hbm,
    filt_ref,
    w_hbm,
    wqkv_hbm,
    out_ref,
    emb,
    wbuf,
    wh,
    halo_tok,
    mask_all,
    frev,
    toep,
    gate_tab,
    feat0,
    win,
    hy,
    send1,
    recv1,
    send_r,
    send_l,
    recv_r,
    recv_l,
    chain_r,
    chain_l,
    own,
    mixed,
    kv,
    keys,
    vals,
    queries,
    scores,
    attended,
    ex_recv,
    gram_send,
    gram_recv,
    emb_sem,
    w_sem,
    wh_sem,
    halo_s,
    halo_r,
    mask_s,
    mask_r,
    s1_s,
    s1_r,
    sr_s,
    sr_r,
    sl_s,
    sl_r,
    a2a_s,
    a2a_r,
    fwd_s,
    fwd_r,
    ex_s,
    ex_r,
    gr_s,
    gr_r,
):
    me = lax.axis_index("seq")
    x = lax.axis_index("mp")
    right = lax.rem(x + 1, mp_n)
    left = lax.rem(x + mp_n - 1, mp_n)
    far = lax.rem(x + 2, mp_n)
    channels = emb.shape[2]
    pairs = 4
    my_pair = me // 8
    my_head = me // 4
    half = lax.rem(me // 2, 2)
    side = lax.rem(me, 2)
    partner = me + 1 - 2 * side
    next_seq = lax.rem(me + 1, seq_n)

    def peer(n):
        return lax.rem(me + n, seq_n)

    barrier = pltpu.get_barrier_semaphore()
    for other in (left, right):
        pl.semaphore_signal(barrier, inc=1, device_id={"mp": other}, device_id_type=MESH)

    def greet(n, carry):
        pl.semaphore_signal(barrier, inc=1, device_id={"seq": peer(n)}, device_id_type=MESH)
        return carry

    lax.fori_loop(1, seq_n, greet, 0)

    emb_copies = [
        pltpu.make_async_copy(emb_hbm.at[i], emb.at[i], emb_sem.at[i]) for i in range(3)
    ]
    for i in (1, 2, 0):
        emb_copies[i].start()
    w_copies = []
    dests = [d for _ in range(pairs) for d in (far, right, left)] + [x] * pairs
    steps = [n for n in range(pairs) for _ in range(3)] + list(range(pairs))
    order = (0, 3, 6, 9, 1, 2, 12, 4, 5, 13, 7, 8, 14, 10, 11, 15)
    for i, (d, n) in enumerate(zip(dests, steps)):
        pair = lax.rem(my_pair + OFFSETS[n], pairs)
        col = pl.multiple_of(d * 1024 + pair * 256, 256)
        w_copies.append(
            pltpu.make_async_copy(w_hbm.at[:, pl.ds(col, 256)], wbuf.at[i], w_sem.at[i])
        )
    for i in order:
        w_copies[i].start()
    wh_copy = pltpu.make_async_copy(wqkv_hbm.at[:, my_head], wh, wh_sem)
    wh_copy.start()

    row_io = lax.broadcasted_iota(jnp.int32, (TOK, TOK), 0)
    col_io = lax.broadcasted_iota(jnp.int32, (TOK, TOK), 1)
    total_io = row_io + col_io
    reverse = jnp.where((total_io == 0) | (total_io == TOK), 1.0, 0.0).astype(BF16)
    frev[...] = dot(filt_ref[...], reverse)

    vocab = emb.shape[1]
    vocab_io = lax.broadcasted_iota(jnp.int32, (vocab, TOK), 0)

    def onehot(ids_ref):
        hot = [
            jnp.where(vocab_io == jnp.broadcast_to(ids_ref[s : s + 1, :], (vocab, TOK)), 1.0, 0.0)
            for s in range(2)
        ]
        return jnp.concatenate(hot, axis=1).astype(BF16)

    emb_copies[1].wait()
    emb_copies[2].wait()
    gate_tab[...] = (emb[1].astype(F32) * emb[2].astype(F32)).astype(BF16)
    own_hot = onehot(tok_ref)
    emb_copies[0].wait()
    feat0[...] = dot_rows(own_hot, emb[0])
    current = dot_rows(own_hot, gate_tab[...]).astype(BF16)
    lane_tiles = channels // 128
    for c in range(lane_tiles):
        for s in range(2):
            win[c, TOK : 2 * TOK, s * 128 : (s + 1) * 128] = current[
                s * TOK : (s + 1) * TOK, c * 128 : (c + 1) * 128
            ]
    pl.semaphore_wait(barrier, seq_n + 1)

    halo = pltpu.make_async_remote_copy(
        src_ref=tok_ref,
        dst_ref=halo_tok,
        send_sem=halo_s,
        recv_sem=halo_r,
        device_id={"seq": next_seq},
        device_id_type=MESH,
    )
    halo.start()

    mask_own = pltpu.make_async_copy(mask_ref, mask_all.at[me], mask_r)
    mask_own.start()

    def send_mask(n, carry):
        pltpu.make_async_remote_copy(
            src_ref=mask_ref,
            dst_ref=mask_all.at[me],
            send_sem=mask_s,
            recv_sem=mask_r,
            device_id={"seq": peer(n)},
            device_id_type=MESH,
        ).start()
        return carry

    lax.fori_loop(1, seq_n, send_mask, 0)

    def build(g, carry):
        base = jnp.broadcast_to(frev[pl.ds(g, 1), :], (TOK, TOK))
        turned = pltpu.roll(base, 0, 1, stride=1, stride_axis=0)
        toep[g, :, 0:TOK] = jnp.where(col_io > row_io, turned, 0.0).astype(BF16)
        toep[g, :, TOK : 2 * TOK] = jnp.where(col_io <= row_io, turned, 0.0).astype(BF16)
        return carry

    lax.fori_loop(0, filt_ref.shape[0], build, 0)

    halo.wait()
    before = dot_rows(onehot(halo_tok), gate_tab[...])
    before = jnp.where(me > 0, before, 0.0).astype(BF16)
    for c in range(lane_tiles):
        for s in range(2):
            win[c, 0:TOK, s * 128 : (s + 1) * 128] = before[
                s * TOK : (s + 1) * TOK, c * 128 : (c + 1) * 128
            ]

    groups = 128 // GROUP
    lane_group = lax.rem(lax.broadcasted_iota(jnp.int32, (TOK, 256), 1), 128) // GROUP

    for c in range(lane_tiles):
        taps = toep[c * groups : (c + 1) * groups].reshape(groups * TOK, 2 * TOK)
        every = dot(taps, win[c])
        conv = every[0:TOK]
        for g in range(1, groups):
            conv = jnp.where(lane_group == g, every[g * TOK : (g + 1) * TOK], conv)
        lanes = pl.ds(c * 128, 128)
        for s in range(2):
            rows = pl.ds(s * TOK, TOK)
            hy[rows, lanes] = (feat0[rows, lanes] * conv[:, s * 128 : (s + 1) * 128]).astype(BF16)

    def part(i):
        w_copies[i].wait()
        return dot(hy[...], wbuf[i])

    def to_side(src, dst, ssem, rsem, other):
        copy = pltpu.make_async_remote_copy(
            src_ref=src,
            dst_ref=dst,
            send_sem=ssem,
            recv_sem=rsem,
            device_id={"mp": other},
            device_id_type=MESH,
        )
        copy.start()
        return copy

    first, second = {}, {}

    def rows_of(s):
        return pl.ds(s * TOK, TOK)

    def send_far(n, s):
        if s == 0:
            p_far = part(3 * n)
            for h in range(2):
                send1[n, h] = p_far[:, h * HEAD : (h + 1) * HEAD].astype(BF16)
        for h, other in ((0, right), (1, left)):
            first[n, h, s] = to_side(
                send1.at[n, h, rows_of(s)],
                recv1.at[n, h, rows_of(s)],
                s1_s.at[n, h, s],
                s1_r.at[n, h, s],
                other,
            )

    def send_right(n, h, s):
        second[n, "r", h, s] = to_side(
            send_r.at[n, h, rows_of(s)],
            recv_l.at[n, h, rows_of(s)],
            sr_s.at[n, h, s],
            sr_r.at[n, h, s],
            right,
        )

    def send_left(n, h, s):
        second[n, "l", h, s] = to_side(
            send_l.at[n, h, rows_of(s)],
            recv_r.at[n, h, rows_of(s)],
            sl_s.at[n, h, s],
            sl_r.at[n, h, s],
            left,
        )

    def send_near(n, s):
        if s == 0:
            p_right = part(3 * n + 1)
            send_r[n, 1] = p_right[:, HEAD:].astype(BF16)
            chain_r[n] = p_right[:, :HEAD]
            p_left = part(3 * n + 2)
            send_l[n, 0] = p_left[:, :HEAD].astype(BF16)
            chain_l[n] = p_left[:, HEAD:]
        send_right(n, 1, s)
        send_left(n, 0, s)

    def send_chain(n, s):
        rows = rows_of(s)
        first[n, 0, s].wait()
        send_r[n, 0, rows] = (chain_r[n, rows] + recv1[n, 0, rows].astype(F32)).astype(BF16)
        send_right(n, 0, s)
        first[n, 1, s].wait()
        send_l[n, 1, rows] = (chain_l[n, rows] + recv1[n, 1, rows].astype(F32)).astype(BF16)
        send_left(n, 1, s)
        if s == 0:
            own[n] = part(12 + n)

    my_y = lax.rem(me // 2, 4)
    other_chip = me + 2 - 4 * half

    def send_rows(n, h, s, target, sem):
        pltpu.make_async_remote_copy(
            src_ref=mixed.at[n, h, s],
            dst_ref=kv.at[me],
            send_sem=a2a_s,
            recv_sem=sem,
            device_id={"seq": target},
            device_id_type=MESH,
        ).start()

    def spread(n, s):
        rows = rows_of(s)
        for key in (("r", 1), ("l", 0), ("r", 0), ("l", 1)):
            second[(n,) + key + (s,)].wait()
        for h in range(2):
            total = own[n, rows, h * HEAD : (h + 1) * HEAD]
            total = total + recv_l[n, h, rows].astype(F32) + recv_r[n, h, rows].astype(F32)
            mixed[n, h, s] = total.astype(BF16)
        base = lax.rem(my_pair + OFFSETS[n], pairs) * 8 + s
        for h in range(2):
            if False:
                near_y = jnp.where(my_y // 2 == h, my_y, 3 - my_y)
                send_rows(n, h, s, base + 2 * near_y, a2a_r.at[n])
            else:
                for a in range(2):
                    target = base + 2 * (2 * h + a)

                    if OFFSETS[n] > 0:
                        send_rows(n, h, s, target, a2a_r.at[n])
                        continue

                    @pl.when(target == me)
                    def _(h=h):
                        pltpu.make_async_copy(mixed.at[n, h, s], kv.at[me], a2a_r.at[n]).start()

                    @pl.when(target != me)
                    def _(h=h, target=target):
                        send_rows(n, h, s, target, a2a_r.at[n])

    def origin(n):
        return lax.rem(my_pair - OFFSETS[n] + pairs, pairs)

    def arrived(n, blocks, sem):
        part_of = kv.at[pl.ds(origin(n) * 8, blocks)]
        pltpu.make_async_copy(part_of, part_of, sem).wait()

    forwards = []

    def forward(n):
        arrived(n, 4, a2a_r.at[n])
        for i, y in enumerate((my_y, 3 - my_y)):
            blocks = kv.at[pl.ds(origin(n) * 8 + 2 * y, 2)]
            copy = pltpu.make_async_remote_copy(
                src_ref=blocks,
                dst_ref=blocks,
                send_sem=fwd_s.at[n, i],
                recv_sem=fwd_r.at[n, i],
                device_id={"seq": other_chip},
                device_id_type=MESH,
            )
            copy.start()
            forwards.append(copy)

    rows_per = CHUNK // TOK

    def project(n):
        arrived(n, 8, a2a_r.at[n])
        for i in range(2):
            c = origin(n) * 2 + i
            rows = kv[pl.ds(c * rows_per, rows_per)].reshape(CHUNK, HEAD)
            keys[c] = dot(rows, wh[1]).astype(BF16)
            vals[c] = lax.dot_general(
                wh[2], rows, (((0,), (1,)), ((), ())), preferred_element_type=F32
            ).astype(BF16)

    halves = [(n, s) for n in range(pairs) for s in range(2)]
    for n, s in halves:
        send_far(n, s)
    ahead = 3
    for n, s in halves[:ahead]:
        send_near(n, s)
        send_chain(n, s)
    for i, (n, s) in enumerate(halves):
        spread(n, s)
        if i + ahead < len(halves):
            send_near(*halves[i + ahead])
            send_chain(*halves[i + ahead])
    wh_copy.wait()
    for n in range(pairs):
        project(n)

    scale = math.log2(math.e) / math.sqrt(HEAD)
    tiles = seq_n * TOK // TILE // 2

    def tile_of(n):
        return 2 * n + lax.rem(n + half, 2)

    for n in range(tiles):
        rows = kv[pl.ds(2 * tile_of(n), 2)].reshape(TILE, HEAD)
        queries[n] = dot(rows, wh[0]).astype(BF16)

    def fold(s):
        return s.reshape(CHUNK // 8, 8, TILE)

    ex_copies = [
        pltpu.make_async_remote_copy(
            src_ref=attended.at[2 * j + 1 - side],
            dst_ref=ex_recv.at[j],
            send_sem=ex_s.at[j],
            recv_sem=ex_r.at[j],
            device_id={"seq": partner},
            device_id_type=MESH,
        )
        for j in range(tiles // 2)
    ]

    def finish(j, gram):
        ex_copies[j].wait()
        tile = tile_of(2 * j + side)
        diff = (attended[2 * j + side] - ex_recv[j]).astype(BF16)
        chosen = jnp.concatenate(
            [mask_all[2 * tile].astype(F32), mask_all[2 * tile + 1].astype(F32)], axis=1
        )
        return gram + dot_lanes((diff.astype(F32) * chosen).astype(BF16), diff)

    pltpu.make_async_copy(mask_all, mask_all, mask_r).wait()
    gram = jnp.zeros((HEAD, HEAD), F32)
    low = jnp.full((8, TILE), MASKED_SCORE, F32)
    best = low
    for n in range(tiles):
        s = dot_lanes(keys[n], queries[n])
        q_pos = tile_of(n) * TILE + lax.broadcasted_iota(jnp.int32, (CHUNK, TILE), 1)
        k_pos = n * CHUNK + lax.broadcasted_iota(jnp.int32, (CHUNK, TILE), 0)
        s = jnp.where(k_pos <= q_pos, s, MASKED_SCORE)
        scores[n % 2, n] = s
        best = jnp.maximum(best, jnp.max(fold(s), axis=0))
        top = jnp.max(best, axis=0, keepdims=True)
        best = low
        row_sum = jnp.zeros((8, TILE), F32)
        acc = jnp.zeros((HEAD, TILE), F32)
        for c in range(n + 1):
            w = jnp.exp2((scores[n % 2, c] - top) * scale)
            row_sum = row_sum + jnp.sum(fold(w), axis=0)
            acc = acc + dot(vals[c], w.astype(BF16))
            if n + 1 < tiles:
                s = dot_lanes(keys[c], queries[n + 1])
                scores[(n + 1) % 2, c] = s
                best = jnp.maximum(best, jnp.max(fold(s), axis=0))
        attended[n] = acc / jnp.sum(row_sum, axis=0, keepdims=True)
        if n % 2 == 1:
            ex_copies[n // 2].start()
        elif n > 0:
            gram = finish(n // 2 - 1, gram)
    gram = finish(tiles // 2 - 1, gram)

    rows_out = HEAD // seq_n
    for i in range(seq_n):
        gram_send[i] = gram[i * rows_out : (i + 1) * rows_out]
    pltpu.make_async_copy(gram_send.at[me], gram_recv.at[me], gr_r).start()

    def send_gram(n, carry):
        target = peer(n)
        pltpu.make_async_remote_copy(
            src_ref=gram_send.at[target],
            dst_ref=gram_recv.at[me],
            send_sem=gr_s,
            recv_sem=gr_r,
            device_id={"seq": target},
            device_id_type=MESH,
        ).start()
        return carry

    lax.fori_loop(1, seq_n, send_gram, 0)

    count = jnp.sum(jnp.sum(mask_all[...].astype(F32), axis=0), axis=1, keepdims=True)
    count = jnp.maximum(count, 1.0)
    pltpu.make_async_copy(gram_recv, gram_recv, gr_r).wait()
    for h in range(out_ref.shape[0]):
        total = gram_recv[4 * h] + gram_recv[4 * h + 1]
        total = total + (gram_recv[4 * h + 2] + gram_recv[4 * h + 3])
        out_ref[h] = total / count

    rest = seq_n - 1
    direct = kv.at[pl.ds(0, 31)]
    pltpu.make_async_copy(direct, direct, a2a_s).wait()
    pltpu.make_async_copy(mask_all.at[pl.ds(0, rest)], mask_all.at[pl.ds(0, rest)], mask_s).wait()
    pltpu.make_async_copy(gram_recv.at[pl.ds(0, rest)], gram_recv.at[pl.ds(0, rest)], gr_s).wait()


def body(seq_n, mp_n, token_ids, pair_mask, embed_table, conv_filter, w_out, w_qkv):
    vocab, _, channels = embed_table.shape
    filters = conv_filter.shape[0]
    heads = w_qkv.shape[1]
    length = seq_n * TOK
    chunks = length // CHUNK
    tiles = length // TILE // 2
    vmem = pl.BlockSpec(memory_space=pltpu.VMEM)
    hbm = pl.BlockSpec(memory_space=pl.ANY)
    dma = pltpu.SemaphoreType.DMA
    scratch = [
        pltpu.VMEM((3, vocab, channels), BF16),
        pltpu.VMEM((16, channels, 256), BF16),
        pltpu.VMEM((3, HEAD, HEAD), BF16),
        pltpu.VMEM((2, TOK), jnp.int32),
        pltpu.VMEM((seq_n, 1, TOK), jnp.int32),
        pltpu.VMEM((filters, TOK), F32),
        pltpu.VMEM((filters, TOK, 2 * TOK), BF16),
        pltpu.VMEM((vocab, channels), BF16),
        pltpu.VMEM((2 * TOK, channels), F32),
        pltpu.VMEM((channels // 128, 2 * TOK, 256), BF16),
        pltpu.VMEM((2 * TOK, channels), BF16),
        pltpu.VMEM((4, 2, 2 * TOK, HEAD), BF16),
        pltpu.VMEM((4, 2, 2 * TOK, HEAD), BF16),
        pltpu.VMEM((4, 2, 2 * TOK, HEAD), BF16),
        pltpu.VMEM((4, 2, 2 * TOK, HEAD), BF16),
        pltpu.VMEM((4, 2, 2 * TOK, HEAD), BF16),
        pltpu.VMEM((4, 2, 2 * TOK, HEAD), BF16),
        pltpu.VMEM((4, 2 * TOK, HEAD), F32),
        pltpu.VMEM((4, 2 * TOK, HEAD), F32),
        pltpu.VMEM((4, 2 * TOK, 2 * HEAD), F32),
        pltpu.VMEM((4, 2, 2, TOK, HEAD), BF16),
        pltpu.VMEM((seq_n, TOK, HEAD), BF16),
        pltpu.VMEM((chunks, CHUNK, HEAD), BF16),
        pltpu.VMEM((chunks, HEAD, CHUNK), BF16),
        pltpu.VMEM((tiles, TILE, HEAD), BF16),
        pltpu.VMEM((2, chunks, CHUNK, TILE), F32),
        pltpu.VMEM((tiles, HEAD, TILE), F32),
        pltpu.VMEM((tiles // 2, HEAD, TILE), F32),
        pltpu.VMEM((seq_n, HEAD // seq_n, HEAD), F32),
        pltpu.VMEM((seq_n, HEAD // seq_n, HEAD), F32),
        dma((3,)),
        dma((16,)),
        dma,
        dma,
        dma,
        dma,
        dma,
        dma((4, 2, 2)),
        dma((4, 2, 2)),
        dma((4, 2, 2)),
        dma((4, 2, 2)),
        dma((4, 2, 2)),
        dma((4, 2, 2)),
        dma,
        dma((4,)),
        dma((3, 2)),
        dma((3, 2)),
        dma((tiles // 2,)),
        dma((tiles // 2,)),
        dma,
        dma,
    ]
    return pl.pallas_call(
        functools.partial(kernel, seq_n, mp_n),
        out_shape=jax.ShapeDtypeStruct((heads, HEAD // seq_n, HEAD), F32),
        in_specs=[vmem, vmem, hbm, vmem, hbm, hbm],
        out_specs=vmem,
        scratch_shapes=scratch,
        compiler_params=pltpu.CompilerParams(
            collective_id=0, has_side_effects=True, vmem_limit_bytes=56 * 1024 * 1024
        ),
        name="steer",
    )(
        token_ids,
        pair_mask.reshape(1, TOK),
        embed_table.transpose(1, 0, 2),
        conv_filter,
        w_out,
        w_qkv,
    )


def solution(mesh):
    in_specs = (
        P(None, "seq"),
        P("seq"),
        P(None, None, "mp"),
        P("mp", None),
        P("mp", None),
        P(None, "mp", None, None),
    )
    out_specs = P("mp", "seq", None)
    run = functools.partial(body, mesh.shape["seq"], mesh.shape["mp"])
    return jax.shard_map(run, mesh=mesh, in_specs=in_specs, out_specs=out_specs, check_vma=False)
```

```python
import functools
import math

import jax
import jax.numpy as jnp
from jax import lax
from jax.experimental import pallas as pl
from jax.experimental.pallas import tpu as pltpu
from jax.sharding import PartitionSpec as P

F32 = jnp.float32
BF16 = jnp.bfloat16
MESH = pl.DeviceIdType.MESH
MASKED_SCORE = -1e30
TOK = 128
HEAD = 128
GROUP = 16
TILE = 256
CHUNK = 512
OFFSETS = (2, 1, 3, 0)


def dot(a, b):
    return jnp.dot(a, b, preferred_element_type=F32)


def dot_rows(a, b):
    return lax.dot_general(a, b, (((0,), (0,)), ((), ())), preferred_element_type=F32)


def dot_lanes(a, b):
    return lax.dot_general(a, b, (((1,), (1,)), ((), ())), preferred_element_type=F32)


def kernel(
    seq_n,
    mp_n,
    tok_ref,
    mask_ref,
    emb_hbm,
    filt_ref,
    w_hbm,
    wqkv_hbm,
    out_ref,
    emb,
    wbuf,
    wh,
    halo_tok,
    mask_all,
    frev,
    toep,
    gate_tab,
    feat0,
    win,
    hy,
    send1,
    recv1,
    send_r,
    send_l,
    recv_r,
    recv_l,
    chain_r,
    chain_l,
    own,
    mixed,
    kv,
    keys,
    vals,
    queries,
    scores,
    attended,
    ex_recv,
    gram_send,
    gram_recv,
    emb_sem,
    w_sem,
    wh_sem,
    halo_s,
    halo_r,
    mask_s,
    mask_r,
    s1_s,
    s1_r,
    sr_s,
    sr_r,
    sl_s,
    sl_r,
    a2a_s,
    a2a_r,
    fwd_s,
    fwd_r,
    ex_s,
    ex_r,
    gr_s,
    gr_r,
):
    me = lax.axis_index("seq")
    x = lax.axis_index("mp")
    right = lax.rem(x + 1, mp_n)
    left = lax.rem(x + mp_n - 1, mp_n)
    far = lax.rem(x + 2, mp_n)
    channels = emb.shape[2]
    pairs = 4
    my_pair = me // 8
    my_head = me // 4
    half = lax.rem(me // 2, 2)
    side = lax.rem(me, 2)
    partner = me + 1 - 2 * side
    next_seq = lax.rem(me + 1, seq_n)

    def peer(n):
        return lax.rem(me + n, seq_n)

    barrier = pltpu.get_barrier_semaphore()
    for other in (left, right):
        pl.semaphore_signal(barrier, inc=1, device_id={"mp": other}, device_id_type=MESH)

    def greet(n, carry):
        pl.semaphore_signal(barrier, inc=1, device_id={"seq": peer(n)}, device_id_type=MESH)
        return carry

    lax.fori_loop(1, seq_n, greet, 0)

    emb_copies = [
        pltpu.make_async_copy(emb_hbm.at[i], emb.at[i], emb_sem.at[i]) for i in range(3)
    ]
    for i in (1, 2, 0):
        emb_copies[i].start()
    w_copies = []
    dests = [d for _ in range(pairs) for d in (far, right, left)] + [x] * pairs
    steps = [n for n in range(pairs) for _ in range(3)] + list(range(pairs))
    order = (0, 3, 6, 9, 1, 2, 12, 4, 5, 13, 7, 8, 14, 10, 11, 15)
    for i, (d, n) in enumerate(zip(dests, steps)):
        pair = lax.rem(my_pair + OFFSETS[n], pairs)
        col = pl.multiple_of(d * 1024 + pair * 256, 256)
        w_copies.append(
            pltpu.make_async_copy(w_hbm.at[:, pl.ds(col, 256)], wbuf.at[i], w_sem.at[i])
        )
    wh_copy = pltpu.make_async_copy(wqkv_hbm.at[:, my_head], wh, wh_sem)
    wh_copy.start()

    row_io = lax.broadcasted_iota(jnp.int32, (TOK, TOK), 0)
    col_io = lax.broadcasted_iota(jnp.int32, (TOK, TOK), 1)
    total_io = row_io + col_io
    reverse = jnp.where((total_io == 0) | (total_io == TOK), 1.0, 0.0).astype(BF16)
    frev[...] = dot(filt_ref[...], reverse)

    vocab = emb.shape[1]
    vocab_io = lax.broadcasted_iota(jnp.int32, (TOK, TOK), 1).astype(F32)

    def onehot(ids_ref):
        rows = []
        for s in range(2):
            ids = jnp.broadcast_to(ids_ref[s : s + 1, :].astype(F32), (TOK, TOK))
            ids = jnp.transpose(ids)
            hot = [jnp.where(ids == vocab_io + v, 1.0, 0.0) for v in range(0, vocab, TOK)]
            rows.append(jnp.concatenate(hot, axis=1))
        return jnp.concatenate(rows, axis=0).astype(BF16)

    emb_copies[1].wait()
    emb_copies[2].wait()
    gate_tab[...] = (emb[1].astype(F32) * emb[2].astype(F32)).astype(BF16)
    own_hot = onehot(tok_ref)
    emb_copies[0].wait()
    feat0[...] = dot(own_hot, emb[0])
    current = dot(own_hot, gate_tab[...]).astype(BF16)
    lane_tiles = channels // 128
    for c in range(lane_tiles):
        for s in range(2):
            win[c, TOK : 2 * TOK, s * 128 : (s + 1) * 128] = current[
                s * TOK : (s + 1) * TOK, c * 128 : (c + 1) * 128
            ]
    pl.semaphore_wait(barrier, seq_n + 1)

    halo = pltpu.make_async_remote_copy(
        src_ref=tok_ref,
        dst_ref=halo_tok,
        send_sem=halo_s,
        recv_sem=halo_r,
        device_id={"seq": next_seq},
        device_id_type=MESH,
    )
    halo.start()
    for i in order:
        w_copies[i].start()

    unroll = 8

    def build(step, carry):
        for i in range(unroll):
            g = step * unroll + i
            base = jnp.broadcast_to(frev[pl.ds(g, 1), :], (TOK, TOK))
            turned = pltpu.roll(base, 0, 1, stride=1, stride_axis=0)
            toep[g, :, 0:TOK] = jnp.where(col_io > row_io, turned, 0.0).astype(BF16)
            toep[g, :, TOK : 2 * TOK] = jnp.where(col_io <= row_io, turned, 0.0).astype(BF16)
        return carry

    lax.fori_loop(0, filt_ref.shape[0] // unroll, build, 0)

    halo.wait()
    before = dot(onehot(halo_tok), gate_tab[...])
    before = jnp.where(me > 0, before, 0.0).astype(BF16)
    for c in range(lane_tiles):
        for s in range(2):
            win[c, 0:TOK, s * 128 : (s + 1) * 128] = before[
                s * TOK : (s + 1) * TOK, c * 128 : (c + 1) * 128
            ]

    groups = 128 // GROUP
    lane_group = lax.rem(lax.broadcasted_iota(jnp.int32, (TOK, 256), 1), 128) // GROUP

    for c in range(lane_tiles):
        taps = toep[c * groups : (c + 1) * groups].reshape(groups * TOK, 2 * TOK)
        every = dot(taps, win[c])
        conv = every[0:TOK]
        for g in range(1, groups):
            conv = jnp.where(lane_group == g, every[g * TOK : (g + 1) * TOK], conv)
        lanes = pl.ds(c * 128, 128)
        for s in range(2):
            rows = pl.ds(s * TOK, TOK)
            hy[rows, lanes] = (feat0[rows, lanes] * conv[:, s * 128 : (s + 1) * 128]).astype(BF16)

    def part(i):
        w_copies[i].wait()
        return dot(hy[...], wbuf[i])

    def to_side(src, dst, ssem, rsem, other):
        copy = pltpu.make_async_remote_copy(
            src_ref=src,
            dst_ref=dst,
            send_sem=ssem,
            recv_sem=rsem,
            device_id={"mp": other},
            device_id_type=MESH,
        )
        copy.start()
        return copy

    first, second = {}, {}

    def rows_of(s):
        return pl.ds(s * TOK, TOK)

    def send_far(n, s):
        if s == 0:
            p_far = part(3 * n)
            for h in range(2):
                send1[n, h] = p_far[:, h * HEAD : (h + 1) * HEAD].astype(BF16)
        for h, other in ((0, right), (1, left)):
            first[n, h, s] = to_side(
                send1.at[n, h, rows_of(s)],
                recv1.at[n, h, rows_of(s)],
                s1_s.at[n, h, s],
                s1_r.at[n, h, s],
                other,
            )

    def send_right(n, h, s):
        second[n, "r", h, s] = to_side(
            send_r.at[n, h, rows_of(s)],
            recv_l.at[n, h, rows_of(s)],
            sr_s.at[n, h, s],
            sr_r.at[n, h, s],
            right,
        )

    def send_left(n, h, s):
        second[n, "l", h, s] = to_side(
            send_l.at[n, h, rows_of(s)],
            recv_r.at[n, h, rows_of(s)],
            sl_s.at[n, h, s],
            sl_r.at[n, h, s],
            left,
        )

    def send_near(n, s):
        if s == 0:
            p_right = part(3 * n + 1)
            send_r[n, 1] = p_right[:, HEAD:].astype(BF16)
            chain_r[n] = p_right[:, :HEAD]
            p_left = part(3 * n + 2)
            send_l[n, 0] = p_left[:, :HEAD].astype(BF16)
            chain_l[n] = p_left[:, HEAD:]
        send_right(n, 1, s)
        send_left(n, 0, s)

    def send_chain(n, s):
        rows = rows_of(s)
        first[n, 0, s].wait()
        send_r[n, 0, rows] = (chain_r[n, rows] + recv1[n, 0, rows].astype(F32)).astype(BF16)
        send_right(n, 0, s)
        first[n, 1, s].wait()
        send_l[n, 1, rows] = (chain_l[n, rows] + recv1[n, 1, rows].astype(F32)).astype(BF16)
        send_left(n, 1, s)
        if s == 0:
            own[n] = part(12 + n)

    my_y = lax.rem(me // 2, 4)
    other_chip = me + 2 - 4 * half

    def send_rows(n, h, s, target, sem):
        pltpu.make_async_remote_copy(
            src_ref=mixed.at[n, h, s],
            dst_ref=kv.at[me],
            send_sem=a2a_s,
            recv_sem=sem,
            device_id={"seq": target},
            device_id_type=MESH,
        ).start()

    def spread(n, s):
        rows = rows_of(s)
        for key in (("r", 1), ("l", 0), ("r", 0), ("l", 1)):
            second[(n,) + key + (s,)].wait()
        for h in range(2):
            total = own[n, rows, h * HEAD : (h + 1) * HEAD]
            total = total + recv_l[n, h, rows].astype(F32) + recv_r[n, h, rows].astype(F32)
            mixed[n, h, s] = total.astype(BF16)
        base = lax.rem(my_pair + OFFSETS[n], pairs) * 8 + s
        for h in range(2):
            if False:
                near_y = jnp.where(my_y // 2 == h, my_y, 3 - my_y)
                send_rows(n, h, s, base + 2 * near_y, a2a_r.at[n])
            else:
                for a in range(2):
                    target = base + 2 * (2 * h + a)

                    if OFFSETS[n] > 0:
                        send_rows(n, h, s, target, a2a_r.at[n])
                        continue

                    @pl.when(target == me)
                    def _(h=h):
                        pltpu.make_async_copy(mixed.at[n, h, s], kv.at[me], a2a_r.at[n]).start()

                    @pl.when(target != me)
                    def _(h=h, target=target):
                        send_rows(n, h, s, target, a2a_r.at[n])

    def origin(n):
        return lax.rem(my_pair - OFFSETS[n] + pairs, pairs)

    def arrived(n, blocks, sem):
        part_of = kv.at[pl.ds(origin(n) * 8, blocks)]
        pltpu.make_async_copy(part_of, part_of, sem).wait()

    forwards = []

    def forward(n):
        arrived(n, 4, a2a_r.at[n])
        for i, y in enumerate((my_y, 3 - my_y)):
            blocks = kv.at[pl.ds(origin(n) * 8 + 2 * y, 2)]
            copy = pltpu.make_async_remote_copy(
                src_ref=blocks,
                dst_ref=blocks,
                send_sem=fwd_s.at[n, i],
                recv_sem=fwd_r.at[n, i],
                device_id={"seq": other_chip},
                device_id_type=MESH,
            )
            copy.start()
            forwards.append(copy)

    rows_per = CHUNK // TOK

    def project(n):
        arrived(n, 8, a2a_r.at[n])
        for i in range(2):
            c = origin(n) * 2 + i
            rows = kv[pl.ds(c * rows_per, rows_per)].reshape(CHUNK, HEAD)
            keys[c] = dot(rows, wh[1]).astype(BF16)
            vals[c] = lax.dot_general(
                wh[2], rows, (((0,), (1,)), ((), ())), preferred_element_type=F32
            ).astype(BF16)

    halves = [(n, s) for n in range(pairs) for s in range(2)]
    for n, s in halves:
        send_far(n, s)

    mask_own = pltpu.make_async_copy(mask_ref, mask_all.at[me], mask_r)
    mask_own.start()

    def send_mask(n, carry):
        pltpu.make_async_remote_copy(
            src_ref=mask_ref,
            dst_ref=mask_all.at[me],
            send_sem=mask_s,
            recv_sem=mask_r,
            device_id={"seq": peer(n)},
            device_id_type=MESH,
        ).start()
        return carry

    lax.fori_loop(1, seq_n, send_mask, 0)

    ahead = len(halves)
    for n, s in halves[:ahead]:
        send_near(n, s)
        send_chain(n, s)
    for i, (n, s) in enumerate(halves):
        spread(n, s)
        if i + ahead < len(halves):
            send_near(*halves[i + ahead])
            send_chain(*halves[i + ahead])
    wh_copy.wait()
    for n in range(pairs):
        project(n)

    scale = math.log2(math.e) / math.sqrt(HEAD)
    tiles = seq_n * TOK // TILE // 2

    def tile_of(n):
        return 2 * n + lax.rem(n + half, 2)

    for n in range(tiles):
        rows = kv[pl.ds(2 * tile_of(n), 2)].reshape(TILE, HEAD)
        queries[n] = dot(rows, wh[0]).astype(BF16)

    def fold(s):
        return s.reshape(CHUNK // 8, 8, TILE)

    ex_copies = [
        pltpu.make_async_remote_copy(
            src_ref=attended.at[2 * j + 1 - side],
            dst_ref=ex_recv.at[j],
            send_sem=ex_s.at[j],
            recv_sem=ex_r.at[j],
            device_id={"seq": partner},
            device_id_type=MESH,
        )
        for j in range(tiles // 2)
    ]

    def finish(j, gram):
        ex_copies[j].wait()
        tile = tile_of(2 * j + side)
        diff = (attended[2 * j + side] - ex_recv[j]).astype(BF16)
        chosen = jnp.concatenate(
            [mask_all[2 * tile].astype(F32), mask_all[2 * tile + 1].astype(F32)], axis=1
        )
        return gram + dot_lanes((diff.astype(F32) * chosen).astype(BF16), diff)

    pltpu.make_async_copy(mask_all, mask_all, mask_r).wait()
    gram = jnp.zeros((HEAD, HEAD), F32)
    low = jnp.full((8, TILE), MASKED_SCORE, F32)
    best = low
    for n in range(tiles):
        s = dot_lanes(keys[n], queries[n])
        q_pos = tile_of(n) * TILE + lax.broadcasted_iota(jnp.int32, (CHUNK, TILE), 1)
        k_pos = n * CHUNK + lax.broadcasted_iota(jnp.int32, (CHUNK, TILE), 0)
        s = jnp.where(k_pos <= q_pos, s, MASKED_SCORE)
        scores[n % 2, n] = s
        best = jnp.maximum(best, jnp.max(fold(s), axis=0))
        top = jnp.max(best, axis=0, keepdims=True)
        best = low
        row_sum = jnp.zeros((8, TILE), F32)
        acc = jnp.zeros((HEAD, TILE), F32)
        for c in range(n + 1):
            w = jnp.exp2((scores[n % 2, c] - top) * scale)
            row_sum = row_sum + jnp.sum(fold(w), axis=0)
            acc = acc + dot(vals[c], w.astype(BF16))
            if n + 1 < tiles:
                s = dot_lanes(keys[c], queries[n + 1])
                scores[(n + 1) % 2, c] = s
                best = jnp.maximum(best, jnp.max(fold(s), axis=0))
        attended[n] = acc / jnp.sum(row_sum, axis=0, keepdims=True)
        if n % 2 == 1:
            ex_copies[n // 2].start()
        elif n > 0:
            gram = finish(n // 2 - 1, gram)
    gram = finish(tiles // 2 - 1, gram)

    rows_out = HEAD // seq_n
    for i in range(seq_n):
        gram_send[i] = gram[i * rows_out : (i + 1) * rows_out]
    pltpu.make_async_copy(gram_send.at[me], gram_recv.at[me], gr_r).start()

    def send_gram(n, carry):
        target = peer(n)
        pltpu.make_async_remote_copy(
            src_ref=gram_send.at[target],
            dst_ref=gram_recv.at[me],
            send_sem=gr_s,
            recv_sem=gr_r,
            device_id={"seq": target},
            device_id_type=MESH,
        ).start()
        return carry

    lax.fori_loop(1, seq_n, send_gram, 0)

    count = jnp.sum(jnp.sum(mask_all[...].astype(F32), axis=0), axis=1, keepdims=True)
    count = jnp.maximum(count, 1.0)
    pltpu.make_async_copy(gram_recv, gram_recv, gr_r).wait()
    for h in range(out_ref.shape[0]):
        total = gram_recv[4 * h] + gram_recv[4 * h + 1]
        total = total + (gram_recv[4 * h + 2] + gram_recv[4 * h + 3])
        out_ref[h] = total / count

    rest = seq_n - 1
    direct = kv.at[pl.ds(0, 31)]
    pltpu.make_async_copy(direct, direct, a2a_s).wait()
    pltpu.make_async_copy(mask_all.at[pl.ds(0, rest)], mask_all.at[pl.ds(0, rest)], mask_s).wait()
    pltpu.make_async_copy(gram_recv.at[pl.ds(0, rest)], gram_recv.at[pl.ds(0, rest)], gr_s).wait()


def body(seq_n, mp_n, token_ids, pair_mask, embed_table, conv_filter, w_out, w_qkv):
    vocab, _, channels = embed_table.shape
    filters = conv_filter.shape[0]
    heads = w_qkv.shape[1]
    length = seq_n * TOK
    chunks = length // CHUNK
    tiles = length // TILE // 2
    vmem = pl.BlockSpec(memory_space=pltpu.VMEM)
    hbm = pl.BlockSpec(memory_space=pl.ANY)
    dma = pltpu.SemaphoreType.DMA
    scratch = [
        pltpu.VMEM((3, vocab, channels), BF16),
        pltpu.VMEM((16, channels, 256), BF16),
        pltpu.VMEM((3, HEAD, HEAD), BF16),
        pltpu.VMEM((2, TOK), jnp.int32),
        pltpu.VMEM((seq_n, 1, TOK), jnp.int32),
        pltpu.VMEM((filters, TOK), F32),
        pltpu.VMEM((filters, TOK, 2 * TOK), BF16),
        pltpu.VMEM((vocab, channels), BF16),
        pltpu.VMEM((2 * TOK, channels), F32),
        pltpu.VMEM((channels // 128, 2 * TOK, 256), BF16),
        pltpu.VMEM((2 * TOK, channels), BF16),
        pltpu.VMEM((4, 2, 2 * TOK, HEAD), BF16),
        pltpu.VMEM((4, 2, 2 * TOK, HEAD), BF16),
        pltpu.VMEM((4, 2, 2 * TOK, HEAD), BF16),
        pltpu.VMEM((4, 2, 2 * TOK, HEAD), BF16),
        pltpu.VMEM((4, 2, 2 * TOK, HEAD), BF16),
        pltpu.VMEM((4, 2, 2 * TOK, HEAD), BF16),
        pltpu.VMEM((4, 2 * TOK, HEAD), F32),
        pltpu.VMEM((4, 2 * TOK, HEAD), F32),
        pltpu.VMEM((4, 2 * TOK, 2 * HEAD), F32),
        pltpu.VMEM((4, 2, 2, TOK, HEAD), BF16),
        pltpu.VMEM((seq_n, TOK, HEAD), BF16),
        pltpu.VMEM((chunks, CHUNK, HEAD), BF16),
        pltpu.VMEM((chunks, HEAD, CHUNK), BF16),
        pltpu.VMEM((tiles, TILE, HEAD), BF16),
        pltpu.VMEM((2, chunks, CHUNK, TILE), F32),
        pltpu.VMEM((tiles, HEAD, TILE), F32),
        pltpu.VMEM((tiles // 2, HEAD, TILE), F32),
        pltpu.VMEM((seq_n, HEAD // seq_n, HEAD), F32),
        pltpu.VMEM((seq_n, HEAD // seq_n, HEAD), F32),
        dma((3,)),
        dma((16,)),
        dma,
        dma,
        dma,
        dma,
        dma,
        dma((4, 2, 2)),
        dma((4, 2, 2)),
        dma((4, 2, 2)),
        dma((4, 2, 2)),
        dma((4, 2, 2)),
        dma((4, 2, 2)),
        dma,
        dma((4,)),
        dma((3, 2)),
        dma((3, 2)),
        dma((tiles // 2,)),
        dma((tiles // 2,)),
        dma,
        dma,
    ]
    return pl.pallas_call(
        functools.partial(kernel, seq_n, mp_n),
        out_shape=jax.ShapeDtypeStruct((heads, HEAD // seq_n, HEAD), F32),
        in_specs=[vmem, vmem, hbm, vmem, hbm, hbm],
        out_specs=vmem,
        scratch_shapes=scratch,
        compiler_params=pltpu.CompilerParams(
            collective_id=0, has_side_effects=True, vmem_limit_bytes=56 * 1024 * 1024
        ),
        name="steer",
    )(
        token_ids,
        pair_mask.reshape(1, TOK),
        embed_table.transpose(1, 0, 2),
        conv_filter,
        w_out,
        w_qkv,
    )


def solution(mesh):
    in_specs = (
        P(None, "seq"),
        P("seq"),
        P(None, None, "mp"),
        P("mp", None),
        P("mp", None),
        P(None, "mp", None, None),
    )
    out_specs = P("mp", "seq", None)
    run = functools.partial(body, mesh.shape["seq"], mesh.shape["mp"])
    return jax.shard_map(run, mesh=mesh, in_specs=in_specs, out_specs=out_specs, check_vma=False)
```

```python
import functools
import math

import jax
import jax.numpy as jnp
from jax import lax
from jax.experimental import pallas as pl
from jax.experimental.pallas import tpu as pltpu
from jax.sharding import PartitionSpec as P

F32 = jnp.float32
BF16 = jnp.bfloat16
MESH = pl.DeviceIdType.MESH
MASKED_SCORE = -1e30
TOK = 128
HEAD = 128
GROUP = 16
TILE = 256
CHUNK = 512
OFFSETS = (2, 1, 3, 0)


def dot(a, b):
    return jnp.dot(a, b, preferred_element_type=F32)


def dot_rows(a, b):
    return lax.dot_general(a, b, (((0,), (0,)), ((), ())), preferred_element_type=F32)


def dot_lanes(a, b):
    return lax.dot_general(a, b, (((1,), (1,)), ((), ())), preferred_element_type=F32)


def kernel(
    seq_n,
    mp_n,
    tok_ref,
    mask_ref,
    emb_hbm,
    filt_ref,
    w_hbm,
    wqkv_hbm,
    out_ref,
    emb,
    wbuf,
    wh,
    halo_tok,
    mask_all,
    frev,
    toep,
    gate_tab,
    feat0,
    win,
    hy,
    send1,
    recv1,
    send_r,
    send_l,
    recv_r,
    recv_l,
    chain_r,
    chain_l,
    own,
    mixed,
    kv,
    keys,
    vals,
    queries,
    scores,
    attended,
    ex_recv,
    gram_send,
    gram_recv,
    emb_sem,
    w_sem,
    wh_sem,
    halo_s,
    halo_r,
    mask_s,
    mask_r,
    s1_s,
    s1_r,
    sr_s,
    sr_r,
    sl_s,
    sl_r,
    a2a_s,
    a2a_r,
    fwd_s,
    fwd_r,
    ex_s,
    ex_r,
    gr_s,
    gr_r,
):
    me = lax.axis_index("seq")
    x = lax.axis_index("mp")
    right = lax.rem(x + 1, mp_n)
    left = lax.rem(x + mp_n - 1, mp_n)
    far = lax.rem(x + 2, mp_n)
    channels = emb.shape[2]
    pairs = 4
    my_pair = me // 8
    my_head = me // 4
    half = lax.rem(me // 2, 2)
    side = lax.rem(me, 2)
    partner = me + 1 - 2 * side
    next_seq = lax.rem(me + 1, seq_n)

    def peer(n):
        return lax.rem(me + n, seq_n)

    barrier = pltpu.get_barrier_semaphore()
    for other in (left, right):
        pl.semaphore_signal(barrier, inc=1, device_id={"mp": other}, device_id_type=MESH)

    def greet(n, carry):
        pl.semaphore_signal(barrier, inc=1, device_id={"seq": peer(n)}, device_id_type=MESH)
        return carry

    lax.fori_loop(1, seq_n, greet, 0)

    emb_copies = [
        pltpu.make_async_copy(emb_hbm.at[i], emb.at[i], emb_sem.at[i]) for i in range(3)
    ]
    for i in (1, 2, 0):
        emb_copies[i].start()
    w_copies = []
    dests = [d for _ in range(pairs) for d in (far, right, left)] + [x] * pairs
    steps = [n for n in range(pairs) for _ in range(3)] + list(range(pairs))
    order = (0, 3, 6, 9, 1, 2, 12, 4, 5, 13, 7, 8, 14, 10, 11, 15)
    for i, (d, n) in enumerate(zip(dests, steps)):
        pair = lax.rem(my_pair + OFFSETS[n], pairs)
        col = pl.multiple_of(d * 1024 + pair * 256, 256)
        w_copies.append(
            pltpu.make_async_copy(w_hbm.at[:, pl.ds(col, 256)], wbuf.at[i], w_sem.at[i])
        )
    wh_copy = pltpu.make_async_copy(wqkv_hbm.at[:, my_head], wh, wh_sem)
    wh_copy.start()

    row_io = lax.broadcasted_iota(jnp.int32, (TOK, TOK), 0)
    col_io = lax.broadcasted_iota(jnp.int32, (TOK, TOK), 1)
    total_io = row_io + col_io
    reverse = jnp.where((total_io == 0) | (total_io == TOK), 1.0, 0.0).astype(BF16)
    frev[...] = dot(filt_ref[...], reverse)

    vocab = emb.shape[1]
    vocab_io = lax.broadcasted_iota(jnp.int32, (TOK, TOK), 1).astype(F32)

    def onehot(ids_ref):
        rows = []
        for s in range(2):
            ids = jnp.broadcast_to(ids_ref[s : s + 1, :].astype(F32), (TOK, TOK))
            ids = jnp.transpose(ids)
            hot = [jnp.where(ids == vocab_io + v, 1.0, 0.0) for v in range(0, vocab, TOK)]
            rows.append(jnp.concatenate(hot, axis=1))
        return jnp.concatenate(rows, axis=0).astype(BF16)

    emb_copies[1].wait()
    emb_copies[2].wait()
    gate_tab[...] = (emb[1].astype(F32) * emb[2].astype(F32)).astype(BF16)
    own_hot = onehot(tok_ref)
    emb_copies[0].wait()
    feat0[...] = dot(own_hot, emb[0])
    current = dot(own_hot, gate_tab[...]).astype(BF16)
    lane_tiles = channels // 128
    for c in range(lane_tiles):
        for s in range(2):
            win[c, TOK : 2 * TOK, s * 128 : (s + 1) * 128] = current[
                s * TOK : (s + 1) * TOK, c * 128 : (c + 1) * 128
            ]
    unroll = 8

    def build(step, carry):
        for i in range(unroll):
            g = step * unroll + i
            base = jnp.broadcast_to(frev[pl.ds(g, 1), :], (TOK, TOK))
            turned = pltpu.roll(base, 0, 1, stride=1, stride_axis=0)
            toep[g, :, 0:TOK] = jnp.where(col_io > row_io, turned, 0.0).astype(BF16)
            toep[g, :, TOK : 2 * TOK] = jnp.where(col_io <= row_io, turned, 0.0).astype(BF16)
        return carry

    build_steps = filt_ref.shape[0] // unroll
    lax.fori_loop(0, build_steps // 2, build, 0)

    pl.semaphore_wait(barrier, seq_n + 1)

    halo = pltpu.make_async_remote_copy(
        src_ref=tok_ref,
        dst_ref=halo_tok,
        send_sem=halo_s,
        recv_sem=halo_r,
        device_id={"seq": next_seq},
        device_id_type=MESH,
    )
    halo.start()
    for i in order:
        w_copies[i].start()

    lax.fori_loop(build_steps // 2, build_steps, build, 0)

    halo.wait()
    before = dot(onehot(halo_tok), gate_tab[...])
    before = jnp.where(me > 0, before, 0.0).astype(BF16)
    for c in range(lane_tiles):
        for s in range(2):
            win[c, 0:TOK, s * 128 : (s + 1) * 128] = before[
                s * TOK : (s + 1) * TOK, c * 128 : (c + 1) * 128
            ]

    groups = 128 // GROUP
    lane_group = lax.rem(lax.broadcasted_iota(jnp.int32, (TOK, 256), 1), 128) // GROUP

    for c in range(lane_tiles):
        taps = toep[c * groups : (c + 1) * groups].reshape(groups * TOK, 2 * TOK)
        every = dot(taps, win[c])
        conv = every[0:TOK]
        for g in range(1, groups):
            conv = jnp.where(lane_group == g, every[g * TOK : (g + 1) * TOK], conv)
        lanes = pl.ds(c * 128, 128)
        for s in range(2):
            rows = pl.ds(s * TOK, TOK)
            hy[rows, lanes] = (feat0[rows, lanes] * conv[:, s * 128 : (s + 1) * 128]).astype(BF16)

    def part(i):
        w_copies[i].wait()
        return dot(hy[...], wbuf[i])

    def to_side(src, dst, ssem, rsem, other):
        copy = pltpu.make_async_remote_copy(
            src_ref=src,
            dst_ref=dst,
            send_sem=ssem,
            recv_sem=rsem,
            device_id={"mp": other},
            device_id_type=MESH,
        )
        copy.start()
        return copy

    first, second = {}, {}

    def rows_of(s):
        return pl.ds(s * TOK, TOK)

    def send_far(n, s):
        if s == 0:
            p_far = part(3 * n)
            for h in range(2):
                send1[n, h] = p_far[:, h * HEAD : (h + 1) * HEAD].astype(BF16)
        for h, other in ((0, right), (1, left)):
            first[n, h, s] = to_side(
                send1.at[n, h, rows_of(s)],
                recv1.at[n, h, rows_of(s)],
                s1_s.at[n, h, s],
                s1_r.at[n, h, s],
                other,
            )

    def send_right(n, h, s):
        second[n, "r", h, s] = to_side(
            send_r.at[n, h, rows_of(s)],
            recv_l.at[n, h, rows_of(s)],
            sr_s.at[n, h, s],
            sr_r.at[n, h, s],
            right,
        )

    def send_left(n, h, s):
        second[n, "l", h, s] = to_side(
            send_l.at[n, h, rows_of(s)],
            recv_r.at[n, h, rows_of(s)],
            sl_s.at[n, h, s],
            sl_r.at[n, h, s],
            left,
        )

    def send_near(n, s):
        if s == 0:
            p_right = part(3 * n + 1)
            send_r[n, 1] = p_right[:, HEAD:].astype(BF16)
            chain_r[n] = p_right[:, :HEAD]
            p_left = part(3 * n + 2)
            send_l[n, 0] = p_left[:, :HEAD].astype(BF16)
            chain_l[n] = p_left[:, HEAD:]
        send_right(n, 1, s)
        send_left(n, 0, s)

    def send_chain(n, s):
        rows = rows_of(s)
        first[n, 0, s].wait()
        send_r[n, 0, rows] = (chain_r[n, rows] + recv1[n, 0, rows].astype(F32)).astype(BF16)
        send_right(n, 0, s)
        first[n, 1, s].wait()
        send_l[n, 1, rows] = (chain_l[n, rows] + recv1[n, 1, rows].astype(F32)).astype(BF16)
        send_left(n, 1, s)
        if s == 0:
            own[n] = part(12 + n)

    my_y = lax.rem(me // 2, 4)
    other_chip = me + 2 - 4 * half

    def send_rows(n, h, s, target, sem):
        pltpu.make_async_remote_copy(
            src_ref=mixed.at[n, h, s],
            dst_ref=kv.at[me],
            send_sem=a2a_s,
            recv_sem=sem,
            device_id={"seq": target},
            device_id_type=MESH,
        ).start()

    def spread(n, s):
        rows = rows_of(s)
        for key in (("r", 1), ("l", 0), ("r", 0), ("l", 1)):
            second[(n,) + key + (s,)].wait()
        for h in range(2):
            total = own[n, rows, h * HEAD : (h + 1) * HEAD]
            total = total + recv_l[n, h, rows].astype(F32) + recv_r[n, h, rows].astype(F32)
            mixed[n, h, s] = total.astype(BF16)
        base = lax.rem(my_pair + OFFSETS[n], pairs) * 8 + s
        for h in range(2):
            if False:
                near_y = jnp.where(my_y // 2 == h, my_y, 3 - my_y)
                send_rows(n, h, s, base + 2 * near_y, a2a_r.at[n])
            else:
                for a in range(2):
                    target = base + 2 * (2 * h + a)

                    if OFFSETS[n] > 0:
                        send_rows(n, h, s, target, a2a_r.at[n])
                        continue

                    @pl.when(target == me)
                    def _(h=h):
                        pltpu.make_async_copy(mixed.at[n, h, s], kv.at[me], a2a_r.at[n]).start()

                    @pl.when(target != me)
                    def _(h=h, target=target):
                        send_rows(n, h, s, target, a2a_r.at[n])

    def origin(n):
        return lax.rem(my_pair - OFFSETS[n] + pairs, pairs)

    def arrived(n, blocks, sem):
        part_of = kv.at[pl.ds(origin(n) * 8, blocks)]
        pltpu.make_async_copy(part_of, part_of, sem).wait()

    forwards = []

    def forward(n):
        arrived(n, 4, a2a_r.at[n])
        for i, y in enumerate((my_y, 3 - my_y)):
            blocks = kv.at[pl.ds(origin(n) * 8 + 2 * y, 2)]
            copy = pltpu.make_async_remote_copy(
                src_ref=blocks,
                dst_ref=blocks,
                send_sem=fwd_s.at[n, i],
                recv_sem=fwd_r.at[n, i],
                device_id={"seq": other_chip},
                device_id_type=MESH,
            )
            copy.start()
            forwards.append(copy)

    rows_per = CHUNK // TOK

    def project(n):
        arrived(n, 8, a2a_r.at[n])
        for i in range(2):
            c = origin(n) * 2 + i
            rows = kv[pl.ds(c * rows_per, rows_per)].reshape(CHUNK, HEAD)
            keys[c] = dot(rows, wh[1]).astype(BF16)
            vals[c] = lax.dot_general(
                wh[2], rows, (((0,), (1,)), ((), ())), preferred_element_type=F32
            ).astype(BF16)

    halves = [(n, s) for n in range(pairs) for s in range(2)]
    for n, s in halves:
        send_far(n, s)

    mask_own = pltpu.make_async_copy(mask_ref, mask_all.at[me], mask_r)
    mask_own.start()

    def send_mask(n, carry):
        pltpu.make_async_remote_copy(
            src_ref=mask_ref,
            dst_ref=mask_all.at[me],
            send_sem=mask_s,
            recv_sem=mask_r,
            device_id={"seq": peer(n)},
            device_id_type=MESH,
        ).start()
        return carry

    lax.fori_loop(1, seq_n, send_mask, 0)

    ahead = len(halves)
    for n, s in halves[:ahead]:
        send_near(n, s)
        send_chain(n, s)
    for i, (n, s) in enumerate(halves):
        spread(n, s)
        if i + ahead < len(halves):
            send_near(*halves[i + ahead])
            send_chain(*halves[i + ahead])
    wh_copy.wait()
    for n in range(pairs):
        project(n)

    scale = math.log2(math.e) / math.sqrt(HEAD)
    tiles = seq_n * TOK // TILE // 2

    def tile_of(n):
        return 2 * n + lax.rem(n + half, 2)

    for n in range(tiles):
        rows = kv[pl.ds(2 * tile_of(n), 2)].reshape(TILE, HEAD)
        queries[n] = dot(rows, wh[0]).astype(BF16)

    def fold(s):
        return s.reshape(CHUNK // 8, 8, TILE)

    ex_copies = [
        pltpu.make_async_remote_copy(
            src_ref=attended.at[2 * j + 1 - side],
            dst_ref=ex_recv.at[j],
            send_sem=ex_s.at[j],
            recv_sem=ex_r.at[j],
            device_id={"seq": partner},
            device_id_type=MESH,
        )
        for j in range(tiles // 2)
    ]

    def finish(j, gram):
        ex_copies[j].wait()
        tile = tile_of(2 * j + side)
        diff = (attended[2 * j + side] - ex_recv[j]).astype(BF16)
        chosen = jnp.concatenate(
            [mask_all[2 * tile].astype(F32), mask_all[2 * tile + 1].astype(F32)], axis=1
        )
        return gram + dot_lanes((diff.astype(F32) * chosen).astype(BF16), diff)

    pltpu.make_async_copy(mask_all, mask_all, mask_r).wait()
    gram = jnp.zeros((HEAD, HEAD), F32)
    low = jnp.full((8, TILE), MASKED_SCORE, F32)
    best = low
    for n in range(tiles):
        s = dot_lanes(keys[n], queries[n])
        q_pos = tile_of(n) * TILE + lax.broadcasted_iota(jnp.int32, (CHUNK, TILE), 1)
        k_pos = n * CHUNK + lax.broadcasted_iota(jnp.int32, (CHUNK, TILE), 0)
        s = jnp.where(k_pos <= q_pos, s, MASKED_SCORE)
        scores[n % 2, n] = s
        best = jnp.maximum(best, jnp.max(fold(s), axis=0))
        top = jnp.max(best, axis=0, keepdims=True)
        best = low
        row_sum = jnp.zeros((8, TILE), F32)
        acc = jnp.zeros((HEAD, TILE), F32)
        for c in range(n + 1):
            w = jnp.exp2((scores[n % 2, c] - top) * scale)
            row_sum = row_sum + jnp.sum(fold(w), axis=0)
            acc = acc + dot(vals[c], w.astype(BF16))
            if n + 1 < tiles:
                s = dot_lanes(keys[c], queries[n + 1])
                scores[(n + 1) % 2, c] = s
                best = jnp.maximum(best, jnp.max(fold(s), axis=0))
        attended[n] = acc / jnp.sum(row_sum, axis=0, keepdims=True)
        if n % 2 == 1:
            ex_copies[n // 2].start()
        elif n > 0:
            gram = finish(n // 2 - 1, gram)
    gram = finish(tiles // 2 - 1, gram)

    rows_out = HEAD // seq_n
    for i in range(seq_n):
        gram_send[i] = gram[i * rows_out : (i + 1) * rows_out]
    pltpu.make_async_copy(gram_send.at[me], gram_recv.at[me], gr_r).start()

    def send_gram(n, carry):
        target = peer(n)
        pltpu.make_async_remote_copy(
            src_ref=gram_send.at[target],
            dst_ref=gram_recv.at[me],
            send_sem=gr_s,
            recv_sem=gr_r,
            device_id={"seq": target},
            device_id_type=MESH,
        ).start()
        return carry

    lax.fori_loop(1, seq_n, send_gram, 0)

    count = jnp.sum(jnp.sum(mask_all[...].astype(F32), axis=0), axis=1, keepdims=True)
    count = jnp.maximum(count, 1.0)
    pltpu.make_async_copy(gram_recv, gram_recv, gr_r).wait()
    for h in range(out_ref.shape[0]):
        total = gram_recv[4 * h] + gram_recv[4 * h + 1]
        total = total + (gram_recv[4 * h + 2] + gram_recv[4 * h + 3])
        out_ref[h] = total / count

    rest = seq_n - 1
    direct = kv.at[pl.ds(0, 31)]
    pltpu.make_async_copy(direct, direct, a2a_s).wait()
    pltpu.make_async_copy(mask_all.at[pl.ds(0, rest)], mask_all.at[pl.ds(0, rest)], mask_s).wait()
    pltpu.make_async_copy(gram_recv.at[pl.ds(0, rest)], gram_recv.at[pl.ds(0, rest)], gr_s).wait()


def body(seq_n, mp_n, token_ids, pair_mask, embed_table, conv_filter, w_out, w_qkv):
    vocab, _, channels = embed_table.shape
    filters = conv_filter.shape[0]
    heads = w_qkv.shape[1]
    length = seq_n * TOK
    chunks = length // CHUNK
    tiles = length // TILE // 2
    vmem = pl.BlockSpec(memory_space=pltpu.VMEM)
    hbm = pl.BlockSpec(memory_space=pl.ANY)
    dma = pltpu.SemaphoreType.DMA
    scratch = [
        pltpu.VMEM((3, vocab, channels), BF16),
        pltpu.VMEM((16, channels, 256), BF16),
        pltpu.VMEM((3, HEAD, HEAD), BF16),
        pltpu.VMEM((2, TOK), jnp.int32),
        pltpu.VMEM((seq_n, 1, TOK), jnp.int32),
        pltpu.VMEM((filters, TOK), F32),
        pltpu.VMEM((filters, TOK, 2 * TOK), BF16),
        pltpu.VMEM((vocab, channels), BF16),
        pltpu.VMEM((2 * TOK, channels), F32),
        pltpu.VMEM((channels // 128, 2 * TOK, 256), BF16),
        pltpu.VMEM((2 * TOK, channels), BF16),
        pltpu.VMEM((4, 2, 2 * TOK, HEAD), BF16),
        pltpu.VMEM((4, 2, 2 * TOK, HEAD), BF16),
        pltpu.VMEM((4, 2, 2 * TOK, HEAD), BF16),
        pltpu.VMEM((4, 2, 2 * TOK, HEAD), BF16),
        pltpu.VMEM((4, 2, 2 * TOK, HEAD), BF16),
        pltpu.VMEM((4, 2, 2 * TOK, HEAD), BF16),
        pltpu.VMEM((4, 2 * TOK, HEAD), F32),
        pltpu.VMEM((4, 2 * TOK, HEAD), F32),
        pltpu.VMEM((4, 2 * TOK, 2 * HEAD), F32),
        pltpu.VMEM((4, 2, 2, TOK, HEAD), BF16),
        pltpu.VMEM((seq_n, TOK, HEAD), BF16),
        pltpu.VMEM((chunks, CHUNK, HEAD), BF16),
        pltpu.VMEM((chunks, HEAD, CHUNK), BF16),
        pltpu.VMEM((tiles, TILE, HEAD), BF16),
        pltpu.VMEM((2, chunks, CHUNK, TILE), F32),
        pltpu.VMEM((tiles, HEAD, TILE), F32),
        pltpu.VMEM((tiles // 2, HEAD, TILE), F32),
        pltpu.VMEM((seq_n, HEAD // seq_n, HEAD), F32),
        pltpu.VMEM((seq_n, HEAD // seq_n, HEAD), F32),
        dma((3,)),
        dma((16,)),
        dma,
        dma,
        dma,
        dma,
        dma,
        dma((4, 2, 2)),
        dma((4, 2, 2)),
        dma((4, 2, 2)),
        dma((4, 2, 2)),
        dma((4, 2, 2)),
        dma((4, 2, 2)),
        dma,
        dma((4,)),
        dma((3, 2)),
        dma((3, 2)),
        dma((tiles // 2,)),
        dma((tiles // 2,)),
        dma,
        dma,
    ]
    return pl.pallas_call(
        functools.partial(kernel, seq_n, mp_n),
        out_shape=jax.ShapeDtypeStruct((heads, HEAD // seq_n, HEAD), F32),
        in_specs=[vmem, vmem, hbm, vmem, hbm, hbm],
        out_specs=vmem,
        scratch_shapes=scratch,
        compiler_params=pltpu.CompilerParams(
            collective_id=0, has_side_effects=True, vmem_limit_bytes=56 * 1024 * 1024
        ),
        name="steer",
    )(
        token_ids,
        pair_mask.reshape(1, TOK),
        embed_table.transpose(1, 0, 2),
        conv_filter,
        w_out,
        w_qkv,
    )


def solution(mesh):
    in_specs = (
        P(None, "seq"),
        P("seq"),
        P(None, None, "mp"),
        P("mp", None),
        P("mp", None),
        P(None, "mp", None, None),
    )
    out_specs = P("mp", "seq", None)
    run = functools.partial(body, mesh.shape["seq"], mesh.shape["mp"])
    return jax.shard_map(run, mesh=mesh, in_specs=in_specs, out_specs=out_specs, check_vma=False)
```
